32 devices in a mesh: groups: 2 (over y), row: 4 (over z), col: 2 (over x), aux: 2 (over core).
Axes of the slice: x: 2, y: 2, z: 4, core: 2. Of those that a mesh axis runs over, the one named last changes fastest.
Arguments:
- amplitudes: bfloat16 [32768, 16384], P(('groups', 'row'), ('col', 'aux')), parts along dimension 0, may hold values from -6 to 6, as said below
- b_factors: bfloat16 [32768, 512], P(('groups', 'row'), ('col', 'aux')), parts along dimension 0, may hold values from -0.25 to 0.25
- fock_blocks: bfloat16 [32768, 256], P(('groups', 'row')), parts along dimension 0, may hold values from -0.375 to 0.375
- occ_index: int32 [32768], P('groups'), parts along dimension 0, may hold values from 0 to 63, as said below
- virt_index: int32 [32768], P('groups'), parts along dimension 0, may hold values from 0 to 255, as said below
- eps_occ: float32 [128], P('groups'), parts along dimension 0, may hold values from -3 to -0.5
- eps_virt: float32 [512], P('groups'), parts along dimension 0, may hold values from 0.5 to 3
Outputs:
- t_next: bfloat16 [32768, 16384], P(('groups', 'row'), ('col', 'aux')), parts along dimension 0
The draws below stay inside these ranges and needn't reach their ends.
There are 2 independent parts, one for each index of `groups`. The reference program is written for one: setup_inputs(seed, part) draws one part's arguments, and reference() takes and returns one part's arrays. A program takes and returns all parts, laid end to end along the dimension named above; each array names one. Nothing has to cross between parts.
Inputs may be any that keep to these rules, and one draw needn't show every extreme that they name: amplitudes is symmetric: amplitudes[p, q] == amplitudes[q, p]. `occ_index`: pairs are occupied-major: all pairs of diagonal block k (p // 256 == k) share one occupied orbital, and distinct blocks have distinct ones. `virt_index`: within each diagonal block the 256 pairs have distinct virtual orbitals, in the same order for every block.
All inputs are finite; a program needn't handle non-finite values.
Results may differ from the reference program's by a relative error of at most 0.0023.
Values may be sent and summed in bfloat16 or wider, within the bound.
A program may use at most 512 MiB of HBM per device.

```python
import jax
import jax.numpy as jnp

NOCC = 64
NVIRT = 256
NAUX = 512
P_SIZE = 16384


def draw_amplitudes(key, part):
    base = jnp.clip(jax.random.normal(key, (P_SIZE, P_SIZE), jnp.float32), -4.0, 4.0)
    return ((base + base.T) * 0.7071).astype(jnp.bfloat16)


def draw_occ_index(key, part):
    labels = jax.random.permutation(jax.random.fold_in(key, 11), NOCC).astype(jnp.int32)
    return jnp.repeat(labels, NVIRT)


def draw_virt_index(key, part):
    labels = jax.random.permutation(jax.random.fold_in(key, 23), NVIRT).astype(jnp.int32)
    return jnp.tile(labels, NOCC)


def levels(key, shape, shards, least, largest):
    factor_of = 1.0
    for position, shards_of in shards:
        draws = jax.random.uniform(jax.random.fold_in(jax.random.fold_in(key, 6), position), (shards_of,), jnp.float32, least / len(shards), largest / len(shards))
        factor_of = factor_of * jnp.repeat(jnp.exp(draws), shape[position] // shards_of).reshape((-1,) + (1,) * (len(shape) - 1 - position))
    return factor_of


def scatter_about(stream_key, shape, deviation, reach, split=(), kind=jnp.bfloat16):
    result = jax.random.normal(stream_key, shape, jnp.float32) * deviation
    if len(split) > 0:
        result = levels(stream_key, shape, split, -0.22, 0.18) * result
    return jnp.clip(result, min=-reach, max=reach).astype(kind)


def setup_inputs(seed: int = 0, part: int = 0) -> dict:
    streams_of = jax.random.split(jax.random.key(seed), 8)
    own_keys = jax.random.split(jax.random.fold_in(streams_of[7], part), 8)
    return {
        "amplitudes": draw_amplitudes(jax.random.fold_in(jax.random.fold_in(streams_of[7], part), 71), part),
        "b_factors": scatter_about(own_keys[1], (P_SIZE, NAUX), ((P_SIZE * NAUX) ** -0.25), 0.25, ((0, 4), (1, 4))),
        "fock_blocks": scatter_about(own_keys[2], (P_SIZE, NVIRT), NVIRT ** -0.5, 0.375, ((0, 4),)),
        "occ_index": draw_occ_index(jax.random.fold_in(jax.random.fold_in(streams_of[7], part), 71), part),
        "virt_index": draw_virt_index(jax.random.fold_in(jax.random.fold_in(streams_of[7], part), 71), part),
        "eps_occ": jnp.clip(jax.random.uniform(own_keys[5], (NOCC,), jnp.float32, -3.0, -0.5), -3.0, -0.5),
        "eps_virt": jnp.clip(jax.random.uniform(own_keys[6], (NVIRT,), jnp.float32, 0.5, 3.0), 0.5, 3.0),
    }


def reference(amplitudes, b_factors, fock_blocks, occ_index, virt_index, eps_occ, eps_virt):
    gmat = jnp.dot(amplitudes, b_factors, preferred_element_type=jnp.float32).astype(jnp.bfloat16)
    blocks = P_SIZE // NVIRT
    tshaped = amplitudes.astype(jnp.float32).reshape(P_SIZE, blocks, NVIRT)
    dshaped = fock_blocks.astype(jnp.float32).reshape(blocks, NVIRT, NVIRT)
    tdprod = jnp.einsum("xkd,kde->xke", tshaped, dshaped).reshape(P_SIZE, P_SIZE)
    zmat = jnp.dot(gmat, b_factors.T, preferred_element_type=jnp.float32) + tdprod
    resmat = zmat + zmat.T
    energy = eps_virt[virt_index] - eps_occ[occ_index]
    delta = energy[:, None] + energy[None, :]
    return (amplitudes.astype(jnp.float32) - resmat / delta).astype(jnp.bfloat16)
```

```python
import functools

import jax
import jax.numpy as jnp
from jax import lax
from jax.experimental import pallas as pl
from jax.experimental.pallas import tpu as pltpu
from jax.sharding import PartitionSpec as P

MESH = pl.DeviceIdType.MESH
LANES = 128
ROW_TILE = 512
COL_TILE = 1024
VMEM_BYTES = 60 * 1024 * 1024


def pair_energy(occ_part, virt_part, eps_occ, eps_virt):
    virt_hit = virt_part[:, None] == jnp.arange(eps_virt.shape[0], dtype=jnp.int32)[None, :]
    occ_hit = occ_part[:, None] == jnp.arange(eps_occ.shape[0], dtype=jnp.int32)[None, :]
    upper = jnp.sum(jnp.where(virt_hit, eps_virt[None, :], 0.0), axis=1)
    lower = jnp.sum(jnp.where(occ_hit, eps_occ[None, :], 0.0), axis=1)
    return upper - lower


def slab(ref, index, width, start, size):
    if width % LANES == 0:
        return ref.at[pl.ds(start, size), pl.ds(pl.multiple_of(index * width, LANES), width)]
    return ref.at[index, pl.ds(start, size)]


def slab_shape(count, rows, width):
    return (rows, count * width) if width % LANES == 0 else (count, rows, width)


def whole(array):
    if array.ndim == 2:
        return array
    count, rows, width = array.shape
    return array.transpose(1, 0, 2).reshape(rows, count * width)


def meet(row, col, aux, rows, cols, auxs):
    barrier = pltpu.get_barrier_semaphore()

    def greet(device):
        pl.semaphore_signal(barrier, inc=1, device_id=device, device_id_type=MESH)

    @pl.when(row > 0)
    def _():
        greet({"row": row - 1})

    @pl.when(row < rows - 1)
    def _():
        greet({"row": row + 1})

    for step in range(1, cols * auxs):
        other = lax.rem(col * auxs + aux + step, cols * auxs)
        greet({"col": other // auxs, "aux": lax.rem(other, auxs)})
    above = jnp.where(row > 0, 1, 0)
    below = jnp.where(row < rows - 1, 1, 0)
    pl.semaphore_wait(barrier, cols * auxs - 1 + above + below)


def exchange_kernel(
    rows, cols, auxs, pieces, loc, along, mine, other,
    zsend, zrecv, csend, crecv, rsend, rrecv, lsem,
):
    row, col, aux = lax.axis_index("row"), lax.axis_index("col"), lax.axis_index("aux")
    count = cols * auxs
    me = col * auxs + aux
    height, width = loc.shape
    size = height // pieces
    meet(row, col, aux, rows, cols, auxs)

    def held(k, p, own):
        return loc.at[pl.ds(p * size, size)] if own else along.at[k, pl.ds(p * size, size)]

    def z_copy(k, p, step, own=False):
        return pltpu.make_async_remote_copy(
            src_ref=held(k, p, own),
            dst_ref=along.at[k, pl.ds(p * size, size)],
            send_sem=zsend.at[(1 - step) // 2, k, p],
            recv_sem=zrecv.at[k, p],
            device_id={"row": row + step},
            device_id_type=MESH,
        )

    def c_copy(k, p, slot, own=False):
        return pltpu.make_async_remote_copy(
            src_ref=held(k, p, own),
            dst_ref=slab(other, slot, width, p * size, size),
            send_sem=csend.at[k, p],
            recv_sem=crecv.at[slot, p],
            device_id={"col": k // auxs, "aux": lax.rem(k, auxs)},
            device_id_type=MESH,
        )

    def c_local(k, p, own=False):
        return pltpu.make_async_copy(
            held(k, p, own), slab(other, me, width, p * size, size), lsem.at[1 + p]
        )

    def dispatch(k, p, own=False):
        @pl.when(k != me)
        def _():
            c_copy(k, p, me, own).start()

        @pl.when(k == me)
        def _():
            c_local(k, p, own).start()

    def r_copy(index, to_col, to_aux, hop, own):
        return pltpu.make_async_remote_copy(
            src_ref=loc if own else slab(mine, index, width, 0, height),
            dst_ref=slab(mine, index, width, 0, height),
            send_sem=rsend.at[hop],
            recv_sem=rrecv.at[index],
            device_id={"col": to_col, "aux": to_aux},
            device_id_type=MESH,
        )

    def r_sends():
        first, second = [], []
        for step in range(1, cols):
            first.append(r_copy(me, lax.rem(col + step, cols), aux, step - 1, True))
        hop = cols - 1
        for step in range(cols):
            from_col = lax.rem(col + step, cols)
            for turn in range(1, auxs):
                second.append((
                    from_col * auxs + aux,
                    r_copy(from_col * auxs + aux, col, lax.rem(aux + turn, auxs), hop, step == 0),
                ))
                hop += 1
        return first, second

    first, second = r_sends()
    for copy in first:
        copy.start()
    for _, copy in second[: auxs - 1]:
        copy.start()
    for p in range(pieces):
        @pl.when(row < rows - 1)
        def _(p=p):
            z_copy(row, p, 1, True).start()

        @pl.when(row > 0)
        def _(p=p):
            z_copy(row, p, -1, True).start()

        dispatch(row, p, True)
    local = pltpu.make_async_copy(loc, slab(mine, me, width, 0, height), lsem.at[0])
    local.start()

    for s in range(1, rows):
        for p in range(pieces):
            @pl.when(row - s >= 0)
            def _(s=s, p=p):
                k = row - s
                z_copy(k, p, 1).wait_recv()

                @pl.when(row < rows - 1)
                def _():
                    z_copy(k, p, 1).start()

                dispatch(k, p)

            @pl.when(row + s < rows)
            def _(s=s, p=p):
                k = row + s
                z_copy(k, p, -1).wait_recv()

                @pl.when(row > 0)
                def _():
                    z_copy(k, p, -1).start()

                dispatch(k, p)
        if s == max(1, rows - 2):
            for index, copy in second[auxs - 1:]:
                r_copy(index, col, aux, 0, False).wait_recv()
                copy.start()

    for step in range(cols):
        from_col = lax.rem(col + step, cols)
        for turn in range(1, auxs):
            index = from_col * auxs + lax.rem(aux + turn, auxs)
            r_copy(index, col, aux, 0, False).wait_recv()
    for copy in first:
        copy.wait_send()
    for _, copy in second:
        copy.wait_send()
    local.wait()
    for step in range(1, count):
        index = lax.rem(me + step, count)
        for p in range(pieces):
            c_copy(me, p, index).wait_recv()
    for k in range(rows):
        for p in range(pieces):
            @pl.when(k != me)
            def _(k=k, p=p):
                c_copy(k, p, me).wait_send()

            @pl.when(k == me)
            def _(k=k, p=p):
                c_local(k, p).wait()

            @pl.when((row < rows - 1) & (row >= k))
            def _(k=k, p=p):
                z_copy(k, p, 1).wait_send()

            @pl.when((row > 0) & (row <= k))
            def _(k=k, p=p):
                z_copy(k, p, -1).wait_send()


def exchange(loc, sizes, collective_id):
    rows, cols, auxs = sizes
    count = cols * auxs
    height, width = loc.shape
    pieces = max(1, 32 // rows)
    shape = slab_shape(count, height, width)
    hops = cols - 1 + cols * (auxs - 1)
    any_space = pl.BlockSpec(memory_space=pl.ANY)
    _, mine, other = pl.pallas_call(
        functools.partial(exchange_kernel, rows, cols, auxs, pieces),
        out_shape=(
            jax.ShapeDtypeStruct((rows, height, width), loc.dtype),
            jax.ShapeDtypeStruct(shape, loc.dtype),
            jax.ShapeDtypeStruct(shape, loc.dtype),
        ),
        in_specs=[any_space],
        out_specs=(any_space, any_space, any_space),
        scratch_shapes=[
            pltpu.SemaphoreType.DMA((2, rows, pieces)),
            pltpu.SemaphoreType.DMA((rows, pieces)),
            pltpu.SemaphoreType.DMA((rows, pieces)),
            pltpu.SemaphoreType.DMA((count, pieces)),
            pltpu.SemaphoreType.DMA((hops,)),
            pltpu.SemaphoreType.DMA((count,)),
            pltpu.SemaphoreType.DMA((1 + pieces,)),
        ],
        compiler_params=pltpu.CompilerParams(
            collective_id=collective_id, has_side_effects=True
        ),
        name="exchange%d" % collective_id,
    )(loc)
    return whole(mine), whole(other)


def reduce_kernel(
    rows, cols, auxs, groups, amps, b_col, fock, total, diag, part, landed, held,
    psend, precv, dsend, drecv, lsem, tsem,
):
    row, col, aux = lax.axis_index("row"), lax.axis_index("col"), lax.axis_index("aux")
    count = cols * auxs
    me = col * auxs + aux
    height, width = total.shape
    size = height // groups
    tile = min(size, 256)

    def fetch(g):
        return pltpu.make_async_copy(
            amps.at[pl.ds(g * size, size)], held.at[g % 2], tsem.at[g % 2]
        )

    fetch(0).start()
    meet(row, col, aux, rows, cols, auxs)

    def p_copy(g, index, slot):
        return pltpu.make_async_remote_copy(
            src_ref=part.at[index, pl.ds(g * size, size)],
            dst_ref=landed.at[slot, pl.ds(g * size, size)],
            send_sem=psend.at[g, index],
            recv_sem=precv.at[g, slot],
            device_id={"col": index // auxs, "aux": lax.rem(index, auxs)},
            device_id_type=MESH,
        )

    def d_copy(p, step, own):
        piece = pl.ds(p * size, size)
        return pltpu.make_async_remote_copy(
            src_ref=fock.at[piece] if own else diag.at[piece],
            dst_ref=diag.at[piece],
            send_sem=dsend.at[(1 - step) // 2, p],
            recv_sem=drecv.at[p],
            device_id={"row": row + step},
            device_id_type=MESH,
        )

    own_diag = pltpu.make_async_copy(fock, diag, lsem.at[0])
    up, down = row < rows - 1, row > 0

    @pl.when(row == me)
    def _():
        own_diag.start()

    for p in range(groups):
        @pl.when((row == me) & up)
        def _(p=p):
            d_copy(p, 1, True).start()

        @pl.when((row == me) & down)
        def _(p=p):
            d_copy(p, -1, True).start()

    def forward(p):
        @pl.when(row > me)
        def _():
            d_copy(p, 1, False).wait_recv()

            @pl.when(up)
            def _():
                d_copy(p, 1, False).start()

        @pl.when(row < me)
        def _():
            d_copy(p, -1, False).wait_recv()

            @pl.when(down)
            def _():
                d_copy(p, -1, False).start()

    ahead = max(groups // 2, 1)
    for g in range(groups):
        if g + 1 < groups:
            fetch(g + 1).start()
        fetch(g).wait()

        @pl.loop(0, size // tile)
        def _(i, g=g):
            at = pl.ds(pl.multiple_of(i * tile, tile), tile)
            to = pl.ds(pl.multiple_of(g * size + i * tile, tile), tile)
            product = jnp.dot(
                held[g % 2, at, :], b_col[...], preferred_element_type=jnp.float32
            ).astype(part.dtype)
            for index in range(count):
                part[index, to, :] = product[:, index * width:(index + 1) * width]

        for step in range(1, count):
            p_copy(g, lax.rem(me + step, count), me).start()
        if g >= ahead:
            forward(g - ahead)
    for p in range(groups - ahead, groups):
        forward(p)

    for g in range(groups):
        for step in range(1, count):
            p_copy(g, me, lax.rem(me + step, count)).wait_recv()

        @pl.loop(0, size // tile)
        def _(i, g=g):
            at = pl.ds(pl.multiple_of(g * size + i * tile, tile), tile)
            acc = part[me, at, :].astype(jnp.float32)
            for step in range(1, count):
                index = lax.rem(me + step, count)
                acc = acc + landed[index, at, :].astype(jnp.float32)
            total[at, :] = acc.astype(total.dtype)

    for g in range(groups):
        for step in range(1, count):
            p_copy(g, lax.rem(me + step, count), me).wait_send()

    @pl.when(row == me)
    def _():
        own_diag.wait()

    for p in range(groups):
        @pl.when(up & (row >= me))
        def _(p=p):
            d_copy(p, 1, False).wait_send()

        @pl.when(down & (row <= me))
        def _(p=p):
            d_copy(p, -1, False).wait_send()


def reduce_rows(amps, b_cols, fock, sizes, collective_id):
    rows, cols, auxs = sizes
    count = cols * auxs
    height, virt = fock.shape
    across = amps.shape[1]
    width = b_cols.shape[1] // count
    groups = max(1, height // 512)
    any_space = pl.BlockSpec(memory_space=pl.ANY)
    in_vmem = pl.BlockSpec(memory_space=pltpu.VMEM)
    return pl.pallas_call(
        functools.partial(reduce_kernel, rows, cols, auxs, groups),
        out_shape=(
            jax.ShapeDtypeStruct((height, width), amps.dtype),
            jax.ShapeDtypeStruct((height, virt), fock.dtype),
        ),
        in_specs=[any_space, in_vmem, any_space],
        out_specs=(in_vmem, any_space),
        scratch_shapes=[
            pltpu.VMEM((count, height, width), amps.dtype),
            pltpu.VMEM((count, height, width), amps.dtype),
            pltpu.VMEM((2, height // groups, across), amps.dtype),
            pltpu.SemaphoreType.DMA((groups, count)),
            pltpu.SemaphoreType.DMA((groups, count)),
            pltpu.SemaphoreType.DMA((2, groups)),
            pltpu.SemaphoreType.DMA((groups,)),
            pltpu.SemaphoreType.DMA((1,)),
            pltpu.SemaphoreType.DMA((2,)),
        ],
        compiler_params=pltpu.CompilerParams(
            collective_id=collective_id, has_side_effects=True, vmem_limit_bytes=VMEM_BYTES
        ),
        name="reduce%d" % collective_id,
    )(amps, b_cols, fock)


def update_kernel(
    virt, tile, t_ref, g_row, b_row, f_row, e_row, g_col, b_col, f_col, e_col, out
):
    high, across = t_ref.shape
    contract = (((1,), (1,)), ((), ()))

    @pl.loop(0, across // tile)
    def _(j):
        base = pl.multiple_of(j * tile, tile)
        at = pl.ds(base, tile)
        acc = lax.dot_general(
            g_row[...], b_col[at, :], contract, preferred_element_type=jnp.float32
        )
        acc = acc + lax.dot_general(
            b_row[...], g_col[at, :], contract, preferred_element_type=jnp.float32
        )
        right = [
            jnp.dot(
                t_ref[:, pl.ds(pl.multiple_of(base + k * virt, virt), virt)],
                f_col[pl.ds(pl.multiple_of(base + k * virt, virt), virt), :],
                preferred_element_type=jnp.float32,
            )
            for k in range(tile // virt)
        ]
        left = [
            lax.dot_general(
                f_row[k * virt:(k + 1) * virt, :],
                t_ref[k * virt:(k + 1) * virt, at],
                (((0,), (0,)), ((), ())),
                preferred_element_type=jnp.float32,
            )
            for k in range(high // virt)
        ]
        acc = acc + jnp.concatenate(right, axis=1) + jnp.concatenate(left, axis=0)
        delta = e_row[...] + e_col[:, at]
        out[:, at] = (t_ref[:, at].astype(jnp.float32) - acc / delta).astype(out.dtype)


def update(amplitudes, g_rows, b_rows, fock, e_rows, g_cols, b_cols, diag, e_cols):
    high, across = amplitudes.shape
    virt = fock.shape[1]
    aux = b_rows.shape[1]
    row_tile, col_tile = min(ROW_TILE, high), min(COL_TILE, across)
    by_row = lambda i: (i, 0)
    fixed = lambda i: (0, 0)
    return pl.pallas_call(
        functools.partial(update_kernel, virt, col_tile),
        out_shape=jax.ShapeDtypeStruct(amplitudes.shape, amplitudes.dtype),
        grid=(high // row_tile,),
        in_specs=[
            pl.BlockSpec((row_tile, across), by_row),
            pl.BlockSpec((row_tile, aux), by_row),
            pl.BlockSpec((row_tile, aux), by_row),
            pl.BlockSpec((row_tile, virt), by_row),
            pl.BlockSpec((row_tile, 1), by_row),
            pl.BlockSpec((across, aux), fixed),
            pl.BlockSpec((across, aux), fixed),
            pl.BlockSpec((across, virt), fixed),
            pl.BlockSpec((1, across), fixed),
        ],
        out_specs=pl.BlockSpec((row_tile, across), by_row),
        compiler_params=pltpu.CompilerParams(vmem_limit_bytes=VMEM_BYTES),
        name="update",
    )(amplitudes, g_rows, b_rows, fock, e_rows, g_cols, b_cols, diag, e_cols)


def staged_body(sizes, amplitudes, b_factors, fock_blocks, occ_index, virt_index, eps_occ, eps_virt):
    height, across = amplitudes.shape
    b_rows, b_cols = exchange(b_factors, sizes, 0)
    g_own, diag = reduce_rows(amplitudes, b_cols, fock_blocks, sizes, 1)
    g_rows, g_cols = exchange(g_own, sizes, 2)

    def energy(start, size):
        return pair_energy(
            lax.dynamic_slice_in_dim(occ_index, start, size),
            lax.dynamic_slice_in_dim(virt_index, start, size),
            eps_occ,
            eps_virt,
        )

    e_rows = energy(lax.axis_index("row") * height, height)
    e_cols = energy(lax.axis_index(("col", "aux")) * across, across)
    return update(
        amplitudes, g_rows, b_rows, fock_blocks, e_rows[:, None],
        g_cols, b_cols, diag, e_cols[None, :],
    )


PIECES = 8
LAG = 2
AHEAD = 3
FUSED_ROWS = 1024
FINISH_ROWS = 512
NT = (((1,), (1,)), ((), ()))
TN = (((0,), (0,)), ((), ()))


def when(*conditions):
    flag = conditions[0]
    for condition in conditions[1:]:
        flag = jnp.logical_and(flag, condition)
    return pl.when(flag)


def residual(t, g_row, b_row, f_row, g_col, b_col, f_col, virt):
    f32 = jnp.float32
    high, wide = t.shape
    acc = lax.dot_general(g_row, b_col, NT, preferred_element_type=f32)
    acc = acc + lax.dot_general(b_row, g_col, NT, preferred_element_type=f32)
    right = [
        jnp.dot(
            t[:, k * virt:(k + 1) * virt], f_col[k * virt:(k + 1) * virt, :],
            preferred_element_type=f32,
        )
        for k in range(wide // virt)
    ]
    left = [
        lax.dot_general(
            f_row[k * virt:(k + 1) * virt, :], t[k * virt:(k + 1) * virt, :], TN,
            preferred_element_type=f32,
        )
        for k in range(high // virt)
    ]
    return acc + jnp.concatenate(right, axis=1) + jnp.concatenate(left, axis=0)


def pair_sums(virt_sum, occ_of, row_block, high, col_block, wide):
    virt = virt_sum.shape[0]
    return jnp.concatenate([
        jnp.concatenate([
            virt_sum - (occ_of(row_block + a) + occ_of(col_block + c))
            for c in range(wide // virt)
        ], axis=1)
        for a in range(high // virt)
    ], axis=0)


def fused_kernel(
    rows, cols, auxs,
    amps, b_loc, fock, occ, virt_at, eps_occ, eps_virt,
    y, grow_out, brow_out, gtail_out, btail_out, dtail_out, vsum_out, along_b, along_g,
    brow, bcol, grow, gcol, frow, dcol, gown, near, near_in, keep, far, far_in,
    t_red, t_upd, obuf, vsum,
    bz_send, bz_recv, bc_send, bc_recv, br_send, br_recv, b_local,
    gz_send, gz_recv, gc_send, gc_recv, gr_send, gr_recv, g_local,
    d_send, d_recv, near_send, near_recv, far_send, far_recv,
    red_sem, upd_sem, out_sem, misc,
):
    row, col, aux = lax.axis_index("row"), lax.axis_index("col"), lax.axis_index("aux")
    count = cols * auxs
    me = col * auxs + aux
    height, width = b_loc.shape
    across = amps.shape[1]
    virt = fock.shape[1]
    size = height // PIECES
    wide = across // PIECES
    tiles = height // FUSED_ROWS
    up, down = row < rows - 1, row > 0
    f32 = jnp.float32

    def part(p):
        return pl.ds(pl.multiple_of(p * size, size), size)

    def at_core(index):
        return {"col": lax.div(index, auxs), "aux": lax.rem(index, auxs)}

    class Exchange:
        def __init__(self, loc, along, mine, other, z_send, z_recv, c_send, c_recv,
                     r_send, r_recv, local):
            self.loc, self.along, self.mine, self.other = loc, along, mine, other
            self.z_send, self.z_recv = z_send, z_recv
            self.c_send, self.c_recv = c_send, c_recv
            self.r_send, self.r_recv, self.local = r_send, r_recv, local

        def held(self, k, p, own):
            return self.loc.at[part(p)] if own else self.along.at[k, part(p)]

        def lane(self, ref, index, p):
            return ref.at[part(p), pl.ds(pl.multiple_of(index * width, LANES), width)]

        def z(self, k, p, step, own=False):
            return pltpu.make_async_remote_copy(
                src_ref=self.held(k, p, own),
                dst_ref=self.along.at[k, part(p)],
                send_sem=self.z_send.at[(1 - step) // 2, k, p],
                recv_sem=self.z_recv.at[k, p],
                device_id={"row": row + step},
                device_id_type=MESH,
            )

        def z_own(self, p):
            @pl.when(up)
            def _():
                self.z(row, p, 1, True).start()

            @pl.when(down)
            def _():
                self.z(row, p, -1, True).start()

        def c(self, k, p, slot, own=False):
            return pltpu.make_async_remote_copy(
                src_ref=self.held(k, p, own),
                dst_ref=self.lane(self.other, slot, p),
                send_sem=self.c_send.at[k, p],
                recv_sem=self.c_recv.at[slot, p],
                device_id=at_core(k),
                device_id_type=MESH,
            )

        def c_here(self, k, p, own=False):
            return pltpu.make_async_copy(
                self.held(k, p, own), self.lane(self.other, me, p), self.local.at[1, p]
            )

        def dispatch(self, k, p, own=False):
            @pl.when(k != me)
            def _():
                self.c(k, p, me, own).start()

            @pl.when(k == me)
            def _():
                self.c_here(k, p, own).start()

        def hop(self, p, s):
            @pl.when(row - s >= 0)
            def _():
                k = row - s
                self.z(k, p, 1).wait_recv()

                @pl.when(up)
                def _():
                    self.z(k, p, 1).start()

                self.dispatch(k, p)

            @pl.when(row + s < rows)
            def _():
                k = row + s
                self.z(k, p, -1).wait_recv()

                @pl.when(down)
                def _():
                    self.z(k, p, -1).start()

                self.dispatch(k, p)

        def r(self, index, p, to_col, to_aux, hop, own):
            return pltpu.make_async_remote_copy(
                src_ref=self.loc.at[part(p)] if own else self.lane(self.mine, index, p),
                dst_ref=self.lane(self.mine, index, p),
                send_sem=self.r_send.at[hop, p],
                recv_sem=self.r_recv.at[index, p],
                device_id={"col": to_col, "aux": to_aux},
                device_id_type=MESH,
            )

        def r_here(self, p):
            return pltpu.make_async_copy(
                self.loc.at[part(p)], self.lane(self.mine, me, p), self.local.at[0, p]
            )

        def r_own(self, p):
            copies = [
                self.r(me, p, lax.rem(col + step, cols), aux, step - 1, True)
                for step in range(1, cols)
            ]
            for turn in range(1, auxs):
                copies.append(
                    self.r(me, p, col, lax.rem(aux + turn, auxs), cols - 2 + turn, True)
                )
            return copies

        def r_start(self, p):
            for copy in self.r_own(p):
                copy.start()
            self.r_here(p).start()

        def r_pass(self, p, step):
            index = lax.rem(col + step, cols) * auxs + aux
            base = cols - 1 + auxs - 1 + (step - 1) * (auxs - 1)
            return index, [
                self.r(index, p, col, lax.rem(aux + turn, auxs), base + turn - 1, False)
                for turn in range(1, auxs)
            ]

        def r_forward(self, p):
            for step in range(1, cols):
                index, copies = self.r_pass(p, step)
                self.r(index, p, col, aux, 0, False).wait_recv()
                for copy in copies:
                    copy.start()

        def r_finish(self, p):
            for step in range(cols):
                for turn in range(1, auxs):
                    index = lax.rem(col + step, cols) * auxs + lax.rem(aux + turn, auxs)
                    self.r(index, p, col, aux, 0, False).wait_recv()
            self.r_here(p).wait()

        def c_finish(self, p):
            for step in range(1, count):
                self.c(me, p, lax.rem(me + step, count)).wait_recv()
            self.c_here(me, p).wait()

        def sent(self, p):
            for copy in self.r_own(p):
                copy.wait_send()
            for step in range(1, cols):
                for copy in self.r_pass(p, step)[1]:
                    copy.wait_send()
            for k in range(rows):
                @pl.when(k != me)
                def _(k=k):
                    self.c(k, p, me).wait_send()

                @when(up, row >= k)
                def _(k=k):
                    self.z(k, p, 1).wait_send()

                @when(down, row <= k)
                def _(k=k):
                    self.z(k, p, -1).wait_send()

    b_move = Exchange(b_loc, along_b, brow, bcol, bz_send, bz_recv, bc_send, bc_recv,
                      br_send, br_recv, b_local)
    g_move = Exchange(gown, along_g, grow, gcol, gz_send, gz_recv, gc_send, gc_recv,
                      gr_send, gr_recv, g_local)

    def red_fetch(g):
        return pltpu.make_async_copy(
            amps.at[part(g)], t_red.at[lax.rem(g, 2)], red_sem.at[lax.rem(g, 2)]
        )

    def tile_rows(t):
        return pl.ds(pl.multiple_of(t * FUSED_ROWS, FUSED_ROWS), FUSED_ROWS)

    def tile_cols(q):
        return pl.ds(pl.multiple_of(q * wide, wide), wide)

    def upd_fetch(q, t):
        return pltpu.make_async_copy(
            amps.at[tile_rows(t), tile_cols(q)], t_upd.at[lax.rem(q, 2), t],
            upd_sem.at[lax.rem(q, 2), t],
        )

    def out_copy(q, t):
        slot = lax.rem(t, 2)
        return pltpu.make_async_copy(
            obuf.at[slot], y.at[tile_rows(t), tile_cols(q)], out_sem.at[slot]
        )

    def d_copy(p, step, own):
        return pltpu.make_async_remote_copy(
            src_ref=fock.at[part(p)] if own else dcol.at[part(p)],
            dst_ref=dcol.at[part(p)],
            send_sem=d_send.at[(1 - step) // 2, p],
            recv_sem=d_recv.at[p],
            device_id={"row": row + step},
            device_id_type=MESH,
        )

    def d_forward(p):
        @pl.when(row > me)
        def _():
            d_copy(p, 1, False).wait_recv()

            @pl.when(up)
            def _():
                d_copy(p, 1, False).start()

        @pl.when(row < me)
        def _():
            d_copy(p, -1, False).wait_recv()

            @pl.when(down)
            def _():
                d_copy(p, -1, False).start()

    f_load = pltpu.make_async_copy(fock, frow, misc.at[0])
    d_here = pltpu.make_async_copy(fock, dcol, misc.at[1])
    f_load.start()
    red_fetch(0).start()
    meet(row, col, aux, rows, cols, auxs)

    for p in range(AHEAD):
        b_move.z_own(p)
        b_move.dispatch(row, p, True)

    lane_at = lax.broadcasted_iota(jnp.int32, (1, virt), 1)

    def place(j, held):
        return jnp.where(lane_at == j, eps_virt[virt_at[j]], held)

    virt_row = lax.fori_loop(0, virt, place, jnp.zeros((1, virt), f32))
    spread = jnp.broadcast_to(virt_row, (virt, virt))
    vsum[...] = spread + spread.T

    @pl.loop(0, PIECES)
    def _(p):
        for s in range(1, rows):
            b_move.hop(p, s)

        @pl.when(p + AHEAD < PIECES)
        def _():
            b_move.z_own(p + AHEAD)
            b_move.dispatch(row, p + AHEAD, True)

        b_move.r_start(p)

        @pl.when(p >= 2)
        def _():
            b_move.r_forward(p - 2)

    @pl.when(row == me)
    def _():
        d_here.start()

        @pl.loop(0, PIECES)
        def _(p):
            @pl.when(up)
            def _():
                d_copy(p, 1, True).start()

            @pl.when(down)
            def _():
                d_copy(p, -1, True).start()

    @pl.loop(0, PIECES)
    def _(p):
        b_move.c_finish(p)

    def near_copy(g, turn, c):
        other = lax.rem(aux + turn, auxs)
        return pltpu.make_async_remote_copy(
            src_ref=near.at[lax.rem(g, 4), c * auxs + other],
            dst_ref=near_in.at[turn - 1, c, part(g)],
            send_sem=near_send.at[turn - 1, c, g],
            recv_sem=near_recv.at[turn - 1, c, g],
            device_id={"col": col, "aux": other},
            device_id_type=MESH,
        )

    def far_copy(g, step):
        return pltpu.make_async_remote_copy(
            src_ref=far.at[step - 1, part(g)],
            dst_ref=far_in.at[step - 1, part(g)],
            send_sem=far_send.at[step - 1, g],
            recv_sem=far_recv.at[step - 1, g],
            device_id={"col": lax.rem(col + step, cols), "aux": aux},
            device_id_type=MESH,
        )

    def near_sum(g, c):
        total = keep[lax.rem(g, 4), c * auxs + aux]
        for turn in range(1, auxs):
            total = total + near_in[turn - 1, c, part(g), :].astype(f32)
        return total

    tile = min(size, 256)
    passes = PIECES // 2

    @pl.loop(0, PIECES + 3)
    def _(j):
        @pl.when(j < PIECES)
        def _():
            @pl.when(j + 1 < PIECES)
            def _():
                red_fetch(j + 1).start()

            red_fetch(j).wait()
            slot = lax.rem(j, 4)

            @pl.loop(0, size // tile)
            def _(i):
                rs = pl.ds(pl.multiple_of(i * tile, tile), tile)
                product = jnp.dot(
                    t_red[lax.rem(j, 2), rs, :], bcol[...], preferred_element_type=f32
                )
                for k in range(count):
                    piece = product[:, k * width:(k + 1) * width]
                    keep[slot, k, rs, :] = piece
                    near[slot, k, rs, :] = piece.astype(near.dtype)

            for turn in range(1, auxs):
                for c in range(cols):
                    near_copy(j, turn, c).start()

        @when(j >= 1, j <= PIECES)
        def _():
            g = j - 1
            for turn in range(1, auxs):
                for c in range(cols):
                    near_copy(g, turn, c).wait_recv()
            for step in range(1, cols):
                far[step - 1, part(g), :] = near_sum(g, lax.rem(col + step, cols)).astype(far.dtype)
                far_copy(g, step).start()

        @pl.when(j >= 3)
        def _():
            g = j - 3
            total = near_sum(g, col)
            for step in range(1, cols):
                far_copy(g, step).wait_recv()
                total = total + far_in[step - 1, part(g), :].astype(f32)
            gown[part(g), :] = total.astype(gown.dtype)
            for turn in range(1, auxs):
                for c in range(cols):
                    near_copy(g, turn, c).wait_send()

            @pl.when(g < AHEAD)
            def _():
                g_move.z_own(g)

            g_move.r_start(g)

        @when(j >= 2, lax.rem(j, 2) == 0)
        def _():
            p = lax.div(j - 2, 2)

            @pl.when(p < passes)
            def _():
                d_forward(p)

        @when(j >= 1, j < 3)
        def _():
            b_move.r_forward(PIECES - 3 + j)

        @when(j >= 3 + passes)
        def _():
            g_move.r_forward(j - 3 - passes)

    g_passed = PIECES - passes
    f_load.wait()
    for t in range(tiles):
        upd_fetch(0, t).start()

    @pl.loop(0, PIECES)
    def _(p):
        b_move.r_finish(p)

    b_out = pltpu.make_async_copy(brow, brow_out, misc.at[2])
    b_out.start()

    def occ_of(block):
        return eps_occ[occ[block * virt]]

    substeps = max(rows - 1, tiles)

    @pl.loop(0, PIECES * substeps)
    def _(n):
        p, t = lax.div(n, substeps), lax.rem(n, substeps)

        @pl.when(t == 0)
        def _():
            g_move.dispatch(row, p, True)

            @pl.when(p + AHEAD < PIECES)
            def _():
                g_move.z_own(p + AHEAD)

            @pl.when(passes + p < PIECES)
            def _():
                d_forward(passes + p)

        @when(p < LAG, t >= 1)
        def _():
            late = g_passed + p * (substeps - 1) + t - 1

            @pl.when(late < PIECES)
            def _():
                g_move.r_forward(late)

        @pl.when(t + 1 < rows)
        def _():
            g_move.hop(p, t + 1)

        q = p - LAG

        @when(q == 0, t == 0)
        def _():
            @pl.loop(0, PIECES)
            def _(i):
                g_move.r_finish(i)

            @pl.when(row == me)
            def _():
                d_here.wait()

        @when(q >= 0, t < tiles)
        def _():
            @pl.when(t == 0)
            def _():
                g_move.c_finish(q)

            @pl.when(q + 1 < PIECES - LAG)
            def _():
                upd_fetch(q + 1, t).start()

            upd_fetch(q, t).wait()

            @pl.when(q * tiles + t >= 2)
            def _():
                out_copy(q, t).wait()

            rs, cs = tile_rows(t), tile_cols(q)
            held = t_upd.at[lax.rem(q, 2), t]
            acc = residual(
                held, grow[rs, :], brow[rs, :], frow.at[rs],
                gcol[cs, :], bcol[cs, :], dcol.at[cs], virt,
            )
            delta = pair_sums(
                vsum[...], occ_of,
                row * (height // virt) + t * (FUSED_ROWS // virt), FUSED_ROWS,
                me * (across // virt) + q * (wide // virt), wide,
            )
            obuf[lax.rem(t, 2)] = (held[...].astype(f32) - acc / delta).astype(obuf.dtype)
            out_copy(q, t).start()

    first = (PIECES - LAG) * wide
    tail = pl.ds(first, LAG * wide)
    outs = [
        pltpu.make_async_copy(grow, grow_out, misc.at[3]),
        pltpu.make_async_copy(bcol.at[tail], btail_out, misc.at[4]),
        pltpu.make_async_copy(dcol.at[tail], dtail_out, misc.at[5]),
        pltpu.make_async_copy(vsum, vsum_out, misc.at[6]),
    ]
    for copy in outs:
        copy.start()

    @pl.loop(PIECES - LAG, PIECES)
    def _(q):
        g_move.c_finish(q)

    g_out = pltpu.make_async_copy(gcol.at[tail], gtail_out, misc.at[7])
    g_out.start()

    @pl.loop(0, PIECES)
    def _(p):
        b_move.sent(p)
        g_move.sent(p)
        for step in range(1, cols):
            far_copy(p, step).wait_send()

        @when(up, row >= me)
        def _():
            d_copy(p, 1, False).wait_send()

        @when(down, row <= me)
        def _():
            d_copy(p, -1, False).wait_send()

    for t in range(2):
        out_copy(0, t).wait()
    b_out.wait()
    for copy in outs:
        copy.wait()
    g_out.wait()


def fused(amps, b_loc, fock, occ, virt_at, eps_occ, eps_virt, sizes):
    rows, cols, auxs = sizes
    count = cols * auxs
    height, across = amps.shape
    width, virt = b_loc.shape[1], fock.shape[1]
    full = count * width
    size, wide = height // PIECES, across // PIECES
    tiles = height // FUSED_ROWS
    tail = LAG * wide
    kind = amps.dtype
    any_space = pl.BlockSpec(memory_space=pl.ANY)
    in_smem = pl.BlockSpec(memory_space=pltpu.SMEM)
    hops = (cols - 1) + (auxs - 1) + (cols - 1) * (auxs - 1)
    dma = pltpu.SemaphoreType.DMA
    exchange_sems = [
        dma((2, rows, PIECES)), dma((rows, PIECES)), dma((rows, PIECES)),
        dma((count, PIECES)), dma((hops, PIECES)), dma((count, PIECES)), dma((2, PIECES)),
    ]
    near = max(auxs - 1, 1)
    far = max(cols - 1, 1)

    def shaped(*shape, dtype=kind):
        return jax.ShapeDtypeStruct(shape, dtype)

    return pl.pallas_call(
        functools.partial(fused_kernel, rows, cols, auxs),
        out_shape=(
            shaped(height, across), shaped(height, full), shaped(height, full),
            shaped(tail, full), shaped(tail, full), shaped(tail, virt),
            shaped(virt, virt, dtype=jnp.float32),
            shaped(rows, height, width), shaped(rows, height, width),
        ),
        in_specs=[any_space] * 3 + [in_smem] * 4,
        out_specs=(any_space,) * 9,
        scratch_shapes=[
            pltpu.VMEM((height, full), kind), pltpu.VMEM((across, full), kind),
            pltpu.VMEM((height, full), kind), pltpu.VMEM((across, full), kind),
            pltpu.VMEM((height, virt), kind), pltpu.VMEM((across, virt), kind),
            pltpu.VMEM((height, width), kind),
            pltpu.VMEM((4, count, size, width), kind),
            pltpu.VMEM((near, cols, height, width), kind),
            pltpu.VMEM((4, count, size, width), jnp.float32),
            pltpu.VMEM((far, height, width), kind),
            pltpu.VMEM((far, height, width), kind),
            pltpu.VMEM((2, size, across), kind),
            pltpu.VMEM((2, tiles, FUSED_ROWS, wide), kind),
            pltpu.VMEM((2, FUSED_ROWS, wide), kind),
            pltpu.VMEM((virt, virt), jnp.float32),
            *exchange_sems, *exchange_sems,
            dma((2, PIECES)), dma((PIECES,)),
            dma((near, cols, PIECES)), dma((near, cols, PIECES)),
            dma((far, PIECES)), dma((far, PIECES)),
            dma((2,)), dma((2, tiles)), dma((2,)), dma((8,)),
        ],
        compiler_params=pltpu.CompilerParams(
            collective_id=3, has_side_effects=True, vmem_limit_bytes=VMEM_BYTES
        ),
        name="fused",
    )(amps, b_loc, fock, occ, virt_at, eps_occ, eps_virt)


def finish_kernel(
    sizes, y, t_ref, g_row, b_row, f_row, g_col, b_col, f_col, vsum, occ, eps_occ,
    out, obuf, held_y, load_sem, store_sem, out_sem,
):
    cols, auxs = sizes
    row = lax.axis_index("row")
    me = lax.axis_index("col") * auxs + lax.axis_index("aux")
    i, steps = pl.program_id(0), pl.num_programs(0)
    high, wide = t_ref.shape
    height, across = out.shape
    virt = f_row.shape[1]
    first = across - wide

    def load_of(n):
        return pltpu.make_async_copy(
            y.at[pl.ds(pl.multiple_of(n * high, high), high), pl.ds(0, first)],
            held_y.at[lax.rem(n, 3)], load_sem.at[lax.rem(n, 3)],
        )

    def store_of(n):
        return pltpu.make_async_copy(
            held_y.at[lax.rem(n, 3)],
            out.at[pl.ds(pl.multiple_of(n * high, high), high), pl.ds(0, first)],
            store_sem.at[lax.rem(n, 3)],
        )

    def out_of(n):
        slot = lax.rem(n, 2)
        return pltpu.make_async_copy(
            obuf.at[slot],
            out.at[pl.ds(pl.multiple_of(n * high, high), high), pl.ds(first, wide)],
            out_sem.at[slot],
        )

    @pl.when(i == 0)
    def _():
        load_of(0).start()
        load_of(1).start()

    @pl.when(i >= 1)
    def _():
        store_of(i - 1).wait()

    @pl.when(i + 2 < steps)
    def _():
        load_of(i + 2).start()

    load_of(i).wait()
    store_of(i).start()

    @pl.when(i >= 2)
    def _():
        out_of(i - 2).wait()

    def occ_of(block):
        return eps_occ[occ[block * virt]]

    slot = lax.rem(i, 2)
    half = wide // 2
    for h in range(2):
        cs = pl.ds(h * half, half)
        held = t_ref.at[:, cs]
        acc = residual(
            held, g_row[...], b_row[...], f_row, g_col[cs, :], b_col[cs, :], f_col.at[cs], virt
        )
        delta = pair_sums(
            vsum[...], occ_of,
            row * (height // virt) + i * (high // virt), high,
            me * (across // virt) + (first + h * half) // virt, half,
        )
        obuf[slot, :, cs] = (held[...].astype(jnp.float32) - acc / delta).astype(obuf.dtype)
    out_of(i).start()

    @pl.when(i == steps - 1)
    def _():
        store_of(i).wait()
        out_of(i - 1).wait()
        out_of(i).wait()


def finish(y, amps, g_rows, b_rows, fock, g_tail, b_tail, d_tail, vsum, occ, eps_occ, sizes):
    height, across = amps.shape
    virt, full, wide = fock.shape[1], g_rows.shape[1], g_tail.shape[0]
    high = FINISH_ROWS
    by_row = lambda i: (i, 0)
    fixed = lambda i: (0, 0)
    last = across // wide - 1
    any_space = pl.BlockSpec(memory_space=pl.ANY)
    in_smem = pl.BlockSpec(memory_space=pltpu.SMEM)
    return pl.pallas_call(
        functools.partial(finish_kernel, sizes[1:]),
        out_shape=jax.ShapeDtypeStruct(amps.shape, amps.dtype),
        grid=(height // high,),
        in_specs=[
            any_space,
            pl.BlockSpec((high, wide), lambda i: (i, last)),
            pl.BlockSpec((high, full), by_row),
            pl.BlockSpec((high, full), by_row),
            pl.BlockSpec((high, virt), by_row),
            pl.BlockSpec((wide, full), fixed),
            pl.BlockSpec((wide, full), fixed),
            pl.BlockSpec((wide, virt), fixed),
            pl.BlockSpec((virt, virt), fixed),
            in_smem,
            in_smem,
        ],
        out_specs=any_space,
        scratch_shapes=[
            pltpu.VMEM((2, high, wide), amps.dtype),
            pltpu.VMEM((3, high, across - wide), amps.dtype),
            pltpu.SemaphoreType.DMA((3,)),
            pltpu.SemaphoreType.DMA((3,)),
            pltpu.SemaphoreType.DMA((2,)),
        ],
        compiler_params=pltpu.CompilerParams(vmem_limit_bytes=VMEM_BYTES),
        name="finish",
    )(y, amps, g_rows, b_rows, fock, g_tail, b_tail, d_tail, vsum, occ, eps_occ)


def fits(sizes, height, across, width, virt):
    rows, cols, auxs = sizes
    return (
        rows == cols * auxs
        and width % LANES == 0
        and height % (4 * FUSED_ROWS) == 0
        and across % (PIECES * virt) == 0
        and rows > 1 and cols > 1 and auxs > 1
    )


def body(sizes, amplitudes, b_factors, fock_blocks, occ_index, virt_index, eps_occ, eps_virt):
    height, across = amplitudes.shape
    if not fits(sizes, height, across, b_factors.shape[1], fock_blocks.shape[1]):
        return staged_body(
            sizes, amplitudes, b_factors, fock_blocks, occ_index, virt_index, eps_occ, eps_virt
        )
    y, g_rows, b_rows, g_tail, b_tail, d_tail, vsum, _, _ = fused(
        amplitudes, b_factors, fock_blocks, occ_index, virt_index, eps_occ, eps_virt, sizes
    )
    return finish(
        y, amplitudes, g_rows, b_rows, fock_blocks, g_tail, b_tail, d_tail, vsum,
        occ_index, eps_occ, sizes,
    )


def solution(mesh):
    in_specs = (
        P(("groups", "row"), ("col", "aux")),
        P(("groups", "row"), ("col", "aux")),
        P(("groups", "row"), None),
        P("groups"),
        P("groups"),
        P("groups"),
        P("groups"),
    )
    out_specs = P(("groups", "row"), ("col", "aux"))
    sizes = (mesh.shape["row"], mesh.shape["col"], mesh.shape["aux"])
    return jax.shard_map(
        functools.partial(body, sizes),
        mesh=mesh, in_specs=in_specs, out_specs=out_specs, check_vma=False,
    )
```

```python
import functools

import jax
import jax.numpy as jnp
from jax import lax
from jax.experimental import pallas as pl
from jax.experimental.pallas import tpu as pltpu
from jax.sharding import PartitionSpec as P

MESH = pl.DeviceIdType.MESH
LANES = 128
ROW_TILE = 512
COL_TILE = 1024
VMEM_BYTES = 60 * 1024 * 1024


def pair_energy(occ_part, virt_part, eps_occ, eps_virt):
    virt_hit = virt_part[:, None] == jnp.arange(eps_virt.shape[0], dtype=jnp.int32)[None, :]
    occ_hit = occ_part[:, None] == jnp.arange(eps_occ.shape[0], dtype=jnp.int32)[None, :]
    upper = jnp.sum(jnp.where(virt_hit, eps_virt[None, :], 0.0), axis=1)
    lower = jnp.sum(jnp.where(occ_hit, eps_occ[None, :], 0.0), axis=1)
    return upper - lower


def slab(ref, index, width, start, size):
    if width % LANES == 0:
        return ref.at[pl.ds(start, size), pl.ds(pl.multiple_of(index * width, LANES), width)]
    return ref.at[index, pl.ds(start, size)]


def slab_shape(count, rows, width):
    return (rows, count * width) if width % LANES == 0 else (count, rows, width)


def whole(array):
    if array.ndim == 2:
        return array
    count, rows, width = array.shape
    return array.transpose(1, 0, 2).reshape(rows, count * width)


def meet(row, col, aux, rows, cols, auxs):
    barrier = pltpu.get_barrier_semaphore()

    def greet(device):
        pl.semaphore_signal(barrier, inc=1, device_id=device, device_id_type=MESH)

    @pl.when(row > 0)
    def _():
        greet({"row": row - 1})

    @pl.when(row < rows - 1)
    def _():
        greet({"row": row + 1})

    for step in range(1, cols * auxs):
        other = lax.rem(col * auxs + aux + step, cols * auxs)
        greet({"col": other // auxs, "aux": lax.rem(other, auxs)})
    above = jnp.where(row > 0, 1, 0)
    below = jnp.where(row < rows - 1, 1, 0)
    pl.semaphore_wait(barrier, cols * auxs - 1 + above + below)


def exchange_kernel(
    rows, cols, auxs, pieces, loc, along, mine, other,
    zsend, zrecv, csend, crecv, rsend, rrecv, lsem,
):
    row, col, aux = lax.axis_index("row"), lax.axis_index("col"), lax.axis_index("aux")
    count = cols * auxs
    me = col * auxs + aux
    height, width = loc.shape
    size = height // pieces
    meet(row, col, aux, rows, cols, auxs)

    def held(k, p, own):
        return loc.at[pl.ds(p * size, size)] if own else along.at[k, pl.ds(p * size, size)]

    def z_copy(k, p, step, own=False):
        return pltpu.make_async_remote_copy(
            src_ref=held(k, p, own),
            dst_ref=along.at[k, pl.ds(p * size, size)],
            send_sem=zsend.at[(1 - step) // 2, k, p],
            recv_sem=zrecv.at[k, p],
            device_id={"row": row + step},
            device_id_type=MESH,
        )

    def c_copy(k, p, slot, own=False):
        return pltpu.make_async_remote_copy(
            src_ref=held(k, p, own),
            dst_ref=slab(other, slot, width, p * size, size),
            send_sem=csend.at[k, p],
            recv_sem=crecv.at[slot, p],
            device_id={"col": k // auxs, "aux": lax.rem(k, auxs)},
            device_id_type=MESH,
        )

    def c_local(k, p, own=False):
        return pltpu.make_async_copy(
            held(k, p, own), slab(other, me, width, p * size, size), lsem.at[1 + p]
        )

    def dispatch(k, p, own=False):
        @pl.when(k != me)
        def _():
            c_copy(k, p, me, own).start()

        @pl.when(k == me)
        def _():
            c_local(k, p, own).start()

    def r_copy(index, to_col, to_aux, hop, own):
        return pltpu.make_async_remote_copy(
            src_ref=loc if own else slab(mine, index, width, 0, height),
            dst_ref=slab(mine, index, width, 0, height),
            send_sem=rsend.at[hop],
            recv_sem=rrecv.at[index],
            device_id={"col": to_col, "aux": to_aux},
            device_id_type=MESH,
        )

    def r_sends():
        first, second = [], []
        for step in range(1, cols):
            first.append(r_copy(me, lax.rem(col + step, cols), aux, step - 1, True))
        hop = cols - 1
        for step in range(cols):
            from_col = lax.rem(col + step, cols)
            for turn in range(1, auxs):
                second.append((
                    from_col * auxs + aux,
                    r_copy(from_col * auxs + aux, col, lax.rem(aux + turn, auxs), hop, step == 0),
                ))
                hop += 1
        return first, second

    first, second = r_sends()
    for copy in first:
        copy.start()
    for _, copy in second[: auxs - 1]:
        copy.start()
    for p in range(pieces):
        @pl.when(row < rows - 1)
        def _(p=p):
            z_copy(row, p, 1, True).start()

        @pl.when(row > 0)
        def _(p=p):
            z_copy(row, p, -1, True).start()

        dispatch(row, p, True)
    local = pltpu.make_async_copy(loc, slab(mine, me, width, 0, height), lsem.at[0])
    local.start()

    for s in range(1, rows):
        for p in range(pieces):
            @pl.when(row - s >= 0)
            def _(s=s, p=p):
                k = row - s
                z_copy(k, p, 1).wait_recv()

                @pl.when(row < rows - 1)
                def _():
                    z_copy(k, p, 1).start()

                dispatch(k, p)

            @pl.when(row + s < rows)
            def _(s=s, p=p):
                k = row + s
                z_copy(k, p, -1).wait_recv()

                @pl.when(row > 0)
                def _():
                    z_copy(k, p, -1).start()

                dispatch(k, p)
        if s == max(1, rows - 2):
            for index, copy in second[auxs - 1:]:
                r_copy(index, col, aux, 0, False).wait_recv()
                copy.start()

    for step in range(cols):
        from_col = lax.rem(col + step, cols)
        for turn in range(1, auxs):
            index = from_col * auxs + lax.rem(aux + turn, auxs)
            r_copy(index, col, aux, 0, False).wait_recv()
    for copy in first:
        copy.wait_send()
    for _, copy in second:
        copy.wait_send()
    local.wait()
    for step in range(1, count):
        index = lax.rem(me + step, count)
        for p in range(pieces):
            c_copy(me, p, index).wait_recv()
    for k in range(rows):
        for p in range(pieces):
            @pl.when(k != me)
            def _(k=k, p=p):
                c_copy(k, p, me).wait_send()

            @pl.when(k == me)
            def _(k=k, p=p):
                c_local(k, p).wait()

            @pl.when((row < rows - 1) & (row >= k))
            def _(k=k, p=p):
                z_copy(k, p, 1).wait_send()

            @pl.when((row > 0) & (row <= k))
            def _(k=k, p=p):
                z_copy(k, p, -1).wait_send()


def exchange(loc, sizes, collective_id):
    rows, cols, auxs = sizes
    count = cols * auxs
    height, width = loc.shape
    pieces = max(1, 32 // rows)
    shape = slab_shape(count, height, width)
    hops = cols - 1 + cols * (auxs - 1)
    any_space = pl.BlockSpec(memory_space=pl.ANY)
    _, mine, other = pl.pallas_call(
        functools.partial(exchange_kernel, rows, cols, auxs, pieces),
        out_shape=(
            jax.ShapeDtypeStruct((rows, height, width), loc.dtype),
            jax.ShapeDtypeStruct(shape, loc.dtype),
            jax.ShapeDtypeStruct(shape, loc.dtype),
        ),
        in_specs=[any_space],
        out_specs=(any_space, any_space, any_space),
        scratch_shapes=[
            pltpu.SemaphoreType.DMA((2, rows, pieces)),
            pltpu.SemaphoreType.DMA((rows, pieces)),
            pltpu.SemaphoreType.DMA((rows, pieces)),
            pltpu.SemaphoreType.DMA((count, pieces)),
            pltpu.SemaphoreType.DMA((hops,)),
            pltpu.SemaphoreType.DMA((count,)),
            pltpu.SemaphoreType.DMA((1 + pieces,)),
        ],
        compiler_params=pltpu.CompilerParams(
            collective_id=collective_id, has_side_effects=True
        ),
        name="exchange%d" % collective_id,
    )(loc)
    return whole(mine), whole(other)


def reduce_kernel(
    rows, cols, auxs, groups, amps, b_col, fock, total, diag, part, landed, held,
    psend, precv, dsend, drecv, lsem, tsem,
):
    row, col, aux = lax.axis_index("row"), lax.axis_index("col"), lax.axis_index("aux")
    count = cols * auxs
    me = col * auxs + aux
    height, width = total.shape
    size = height // groups
    tile = min(size, 256)

    def fetch(g):
        return pltpu.make_async_copy(
            amps.at[pl.ds(g * size, size)], held.at[g % 2], tsem.at[g % 2]
        )

    fetch(0).start()
    meet(row, col, aux, rows, cols, auxs)

    def p_copy(g, index, slot):
        return pltpu.make_async_remote_copy(
            src_ref=part.at[index, pl.ds(g * size, size)],
            dst_ref=landed.at[slot, pl.ds(g * size, size)],
            send_sem=psend.at[g, index],
            recv_sem=precv.at[g, slot],
            device_id={"col": index // auxs, "aux": lax.rem(index, auxs)},
            device_id_type=MESH,
        )

    def d_copy(p, step, own):
        piece = pl.ds(p * size, size)
        return pltpu.make_async_remote_copy(
            src_ref=fock.at[piece] if own else diag.at[piece],
            dst_ref=diag.at[piece],
            send_sem=dsend.at[(1 - step) // 2, p],
            recv_sem=drecv.at[p],
            device_id={"row": row + step},
            device_id_type=MESH,
        )

    own_diag = pltpu.make_async_copy(fock, diag, lsem.at[0])
    up, down = row < rows - 1, row > 0

    @pl.when(row == me)
    def _():
        own_diag.start()

    for p in range(groups):
        @pl.when((row == me) & up)
        def _(p=p):
            d_copy(p, 1, True).start()

        @pl.when((row == me) & down)
        def _(p=p):
            d_copy(p, -1, True).start()

    def forward(p):
        @pl.when(row > me)
        def _():
            d_copy(p, 1, False).wait_recv()

            @pl.when(up)
            def _():
                d_copy(p, 1, False).start()

        @pl.when(row < me)
        def _():
            d_copy(p, -1, False).wait_recv()

            @pl.when(down)
            def _():
                d_copy(p, -1, False).start()

    ahead = max(groups // 2, 1)
    for g in range(groups):
        if g + 1 < groups:
            fetch(g + 1).start()
        fetch(g).wait()

        @pl.loop(0, size // tile)
        def _(i, g=g):
            at = pl.ds(pl.multiple_of(i * tile, tile), tile)
            to = pl.ds(pl.multiple_of(g * size + i * tile, tile), tile)
            product = jnp.dot(
                held[g % 2, at, :], b_col[...], preferred_element_type=jnp.float32
            ).astype(part.dtype)
            for index in range(count):
                part[index, to, :] = product[:, index * width:(index + 1) * width]

        for step in range(1, count):
            p_copy(g, lax.rem(me + step, count), me).start()
        if g >= ahead:
            forward(g - ahead)
    for p in range(groups - ahead, groups):
        forward(p)

    for g in range(groups):
        for step in range(1, count):
            p_copy(g, me, lax.rem(me + step, count)).wait_recv()

        @pl.loop(0, size // tile)
        def _(i, g=g):
            at = pl.ds(pl.multiple_of(g * size + i * tile, tile), tile)
            acc = part[me, at, :].astype(jnp.float32)
            for step in range(1, count):
                index = lax.rem(me + step, count)
                acc = acc + landed[index, at, :].astype(jnp.float32)
            total[at, :] = acc.astype(total.dtype)

    for g in range(groups):
        for step in range(1, count):
            p_copy(g, lax.rem(me + step, count), me).wait_send()

    @pl.when(row == me)
    def _():
        own_diag.wait()

    for p in range(groups):
        @pl.when(up & (row >= me))
        def _(p=p):
            d_copy(p, 1, False).wait_send()

        @pl.when(down & (row <= me))
        def _(p=p):
            d_copy(p, -1, False).wait_send()


def reduce_rows(amps, b_cols, fock, sizes, collective_id):
    rows, cols, auxs = sizes
    count = cols * auxs
    height, virt = fock.shape
    across = amps.shape[1]
    width = b_cols.shape[1] // count
    groups = max(1, height // 512)
    any_space = pl.BlockSpec(memory_space=pl.ANY)
    in_vmem = pl.BlockSpec(memory_space=pltpu.VMEM)
    return pl.pallas_call(
        functools.partial(reduce_kernel, rows, cols, auxs, groups),
        out_shape=(
            jax.ShapeDtypeStruct((height, width), amps.dtype),
            jax.ShapeDtypeStruct((height, virt), fock.dtype),
        ),
        in_specs=[any_space, in_vmem, any_space],
        out_specs=(in_vmem, any_space),
        scratch_shapes=[
            pltpu.VMEM((count, height, width), amps.dtype),
            pltpu.VMEM((count, height, width), amps.dtype),
            pltpu.VMEM((2, height // groups, across), amps.dtype),
            pltpu.SemaphoreType.DMA((groups, count)),
            pltpu.SemaphoreType.DMA((groups, count)),
            pltpu.SemaphoreType.DMA((2, groups)),
            pltpu.SemaphoreType.DMA((groups,)),
            pltpu.SemaphoreType.DMA((1,)),
            pltpu.SemaphoreType.DMA((2,)),
        ],
        compiler_params=pltpu.CompilerParams(
            collective_id=collective_id, has_side_effects=True, vmem_limit_bytes=VMEM_BYTES
        ),
        name="reduce%d" % collective_id,
    )(amps, b_cols, fock)


def update_kernel(
    virt, tile, t_ref, g_row, b_row, f_row, e_row, g_col, b_col, f_col, e_col, out
):
    high, across = t_ref.shape
    contract = (((1,), (1,)), ((), ()))

    @pl.loop(0, across // tile)
    def _(j):
        base = pl.multiple_of(j * tile, tile)
        at = pl.ds(base, tile)
        acc = lax.dot_general(
            g_row[...], b_col[at, :], contract, preferred_element_type=jnp.float32
        )
        acc = acc + lax.dot_general(
            b_row[...], g_col[at, :], contract, preferred_element_type=jnp.float32
        )
        right = [
            jnp.dot(
                t_ref[:, pl.ds(pl.multiple_of(base + k * virt, virt), virt)],
                f_col[pl.ds(pl.multiple_of(base + k * virt, virt), virt), :],
                preferred_element_type=jnp.float32,
            )
            for k in range(tile // virt)
        ]
        left = [
            lax.dot_general(
                f_row[k * virt:(k + 1) * virt, :],
                t_ref[k * virt:(k + 1) * virt, at],
                (((0,), (0,)), ((), ())),
                preferred_element_type=jnp.float32,
            )
            for k in range(high // virt)
        ]
        acc = acc + jnp.concatenate(right, axis=1) + jnp.concatenate(left, axis=0)
        delta = e_row[...] + e_col[:, at]
        out[:, at] = (t_ref[:, at].astype(jnp.float32) - acc / delta).astype(out.dtype)


def update(amplitudes, g_rows, b_rows, fock, e_rows, g_cols, b_cols, diag, e_cols):
    high, across = amplitudes.shape
    virt = fock.shape[1]
    aux = b_rows.shape[1]
    row_tile, col_tile = min(ROW_TILE, high), min(COL_TILE, across)
    by_row = lambda i: (i, 0)
    fixed = lambda i: (0, 0)
    return pl.pallas_call(
        functools.partial(update_kernel, virt, col_tile),
        out_shape=jax.ShapeDtypeStruct(amplitudes.shape, amplitudes.dtype),
        grid=(high // row_tile,),
        in_specs=[
            pl.BlockSpec((row_tile, across), by_row),
            pl.BlockSpec((row_tile, aux), by_row),
            pl.BlockSpec((row_tile, aux), by_row),
            pl.BlockSpec((row_tile, virt), by_row),
            pl.BlockSpec((row_tile, 1), by_row),
            pl.BlockSpec((across, aux), fixed),
            pl.BlockSpec((across, aux), fixed),
            pl.BlockSpec((across, virt), fixed),
            pl.BlockSpec((1, across), fixed),
        ],
        out_specs=pl.BlockSpec((row_tile, across), by_row),
        compiler_params=pltpu.CompilerParams(vmem_limit_bytes=VMEM_BYTES),
        name="update",
    )(amplitudes, g_rows, b_rows, fock, e_rows, g_cols, b_cols, diag, e_cols)


def staged_body(sizes, amplitudes, b_factors, fock_blocks, occ_index, virt_index, eps_occ, eps_virt):
    height, across = amplitudes.shape
    b_rows, b_cols = exchange(b_factors, sizes, 0)
    g_own, diag = reduce_rows(amplitudes, b_cols, fock_blocks, sizes, 1)
    g_rows, g_cols = exchange(g_own, sizes, 2)

    def energy(start, size):
        return pair_energy(
            lax.dynamic_slice_in_dim(occ_index, start, size),
            lax.dynamic_slice_in_dim(virt_index, start, size),
            eps_occ,
            eps_virt,
        )

    e_rows = energy(lax.axis_index("row") * height, height)
    e_cols = energy(lax.axis_index(("col", "aux")) * across, across)
    return update(
        amplitudes, g_rows, b_rows, fock_blocks, e_rows[:, None],
        g_cols, b_cols, diag, e_cols[None, :],
    )


PIECES = 8
LAG = 2
AHEAD = 4
EARLY = PIECES // 2
FUSED_ROWS = 1024
SCRATCH_BYTES = 19 * 1024 * 1024
NT = (((1,), (1,)), ((), ()))
TN = (((0,), (0,)), ((), ()))


def when(*conditions):
    flag = conditions[0]
    for condition in conditions[1:]:
        flag = jnp.logical_and(flag, condition)
    return pl.when(flag)


def residual(t, g_row, b_row, f_row, g_col, b_col, f_col, virt):
    f32 = jnp.float32
    high, wide = t.shape
    acc = lax.dot_general(g_row, b_col, NT, preferred_element_type=f32)
    acc = acc + lax.dot_general(b_row, g_col, NT, preferred_element_type=f32)
    right = [
        jnp.dot(
            t[:, k * virt:(k + 1) * virt], f_col[k * virt:(k + 1) * virt, :],
            preferred_element_type=f32,
        )
        for k in range(wide // virt)
    ]
    left = [
        lax.dot_general(
            f_row[k * virt:(k + 1) * virt, :], t[k * virt:(k + 1) * virt, :], TN,
            preferred_element_type=f32,
        )
        for k in range(high // virt)
    ]
    return acc + jnp.concatenate(right, axis=1) + jnp.concatenate(left, axis=0)


def pair_sums(virt_sum, occ_of, row_block, high, col_block, wide):
    virt = virt_sum.shape[0]
    return jnp.concatenate([
        jnp.concatenate([
            virt_sum - (occ_of(row_block + a) + occ_of(col_block + c))
            for c in range(wide // virt)
        ], axis=1)
        for a in range(high // virt)
    ], axis=0)


def meet_all(row, col, aux, rows, cols, auxs):
    barrier = pltpu.get_barrier_semaphore()
    for step in range(1, rows):
        pl.semaphore_signal(
            barrier, inc=1, device_id={"row": lax.rem(row + step, rows)}, device_id_type=MESH
        )
    for step in range(1, cols * auxs):
        other = lax.rem(col * auxs + aux + step, cols * auxs)
        pl.semaphore_signal(
            barrier, inc=1, device_id={"col": other // auxs, "aux": lax.rem(other, auxs)},
            device_id_type=MESH,
        )
    pl.semaphore_wait(barrier, rows + cols * auxs - 2)


def fused_kernel(
    rows, cols, auxs,
    amps, b_loc, fock, occ, virt_at, eps_occ, eps_virt,
    y, grow, brow, gcol, bcol, frow, dcol, vsum, along_b, along_g,
    gown, near, near_in, keep, far, far_in,
    bz_send, bz_recv, bc_send, bc_recv, br_send, br_recv, b_local,
    gz_send, gz_recv, gc_send, gc_recv, gr_send, gr_recv, g_local,
    d_send, d_recv, near_send, near_recv, far_send, far_recv,
    red_sem, upd_sem, misc,
):
    row, col, aux = lax.axis_index("row"), lax.axis_index("col"), lax.axis_index("aux")
    count = cols * auxs
    me = col * auxs + aux
    height, width = b_loc.shape
    across = amps.shape[1]
    virt = fock.shape[1]
    size = height // PIECES
    wide = across // PIECES
    tiles = height // FUSED_ROWS
    up, down = row < rows - 1, row > 0
    f32 = jnp.float32

    def part(p):
        return pl.ds(pl.multiple_of(p * size, size), size)

    def at_core(index):
        return {"col": lax.div(index, auxs), "aux": lax.rem(index, auxs)}

    class Exchange:
        def __init__(self, loc, along, mine, other, z_send, z_recv, c_send, c_recv,
                     r_send, r_recv, local):
            self.loc, self.along, self.mine, self.other = loc, along, mine, other
            self.z_send, self.z_recv = z_send, z_recv
            self.c_send, self.c_recv = c_send, c_recv
            self.r_send, self.r_recv, self.local = r_send, r_recv, local

        def held(self, k, p, own):
            return self.loc.at[part(p)] if own else self.along.at[k, part(p)]

        def lane(self, ref, index, p):
            return ref.at[part(p), pl.ds(pl.multiple_of(index * width, LANES), width)]

        def z(self, k, p, step, own=False):
            return pltpu.make_async_remote_copy(
                src_ref=self.held(k, p, own),
                dst_ref=self.along.at[k, part(p)],
                send_sem=self.z_send.at[(1 - step) // 2, k, p],
                recv_sem=self.z_recv.at[k, p],
                device_id={"row": row + step},
                device_id_type=MESH,
            )

        def z_own(self, p):
            @pl.when(up)
            def _():
                self.z(row, p, 1, True).start()

            @pl.when(down)
            def _():
                self.z(row, p, -1, True).start()

        def c(self, k, p, slot, own=False):
            return pltpu.make_async_remote_copy(
                src_ref=self.held(k, p, own),
                dst_ref=self.lane(self.other, slot, p),
                send_sem=self.c_send.at[k, p],
                recv_sem=self.c_recv.at[slot, p],
                device_id=at_core(k),
                device_id_type=MESH,
            )

        def c_here(self, k, p, own=False):
            return pltpu.make_async_copy(
                self.held(k, p, own), self.lane(self.other, me, p), self.local.at[1, p]
            )

        def dispatch(self, k, p, own=False):
            @pl.when(k != me)
            def _():
                self.c(k, p, me, own).start()

            @pl.when(k == me)
            def _():
                self.c_here(k, p, own).start()

        def hop(self, p, s):
            @pl.when(row - s >= 0)
            def _():
                k = row - s
                self.z(k, p, 1).wait_recv()

                @pl.when(up)
                def _():
                    self.z(k, p, 1).start()

                self.dispatch(k, p)

            @pl.when(row + s < rows)
            def _():
                k = row + s
                self.z(k, p, -1).wait_recv()

                @pl.when(down)
                def _():
                    self.z(k, p, -1).start()

                self.dispatch(k, p)

        def r(self, index, p, to_col, to_aux, hop, own):
            return pltpu.make_async_remote_copy(
                src_ref=self.loc.at[part(p)] if own else self.lane(self.mine, index, p),
                dst_ref=self.lane(self.mine, index, p),
                send_sem=self.r_send.at[hop, p],
                recv_sem=self.r_recv.at[index, p],
                device_id={"col": to_col, "aux": to_aux},
                device_id_type=MESH,
            )

        def r_here(self, p):
            return pltpu.make_async_copy(
                self.loc.at[part(p)], self.lane(self.mine, me, p), self.local.at[0, p]
            )

        def r_own(self, p):
            copies = [
                self.r(me, p, lax.rem(col + step, cols), aux, step - 1, True)
                for step in range(1, cols)
            ]
            for turn in range(1, auxs):
                copies.append(
                    self.r(me, p, col, lax.rem(aux + turn, auxs), cols - 2 + turn, True)
                )
            return copies

        def r_start(self, p):
            for copy in self.r_own(p):
                copy.start()
            self.r_here(p).start()

        def r_pass(self, p, step):
            index = lax.rem(col + step, cols) * auxs + aux
            base = cols - 1 + auxs - 1 + (step - 1) * (auxs - 1)
            return index, [
                self.r(index, p, col, lax.rem(aux + turn, auxs), base + turn - 1, False)
                for turn in range(1, auxs)
            ]

        def r_forward(self, p):
            for step in range(1, cols):
                index, copies = self.r_pass(p, step)
                self.r(index, p, col, aux, 0, False).wait_recv()
                for copy in copies:
                    copy.start()

        def r_finish(self, p):
            for step in range(cols):
                for turn in range(1, auxs):
                    index = lax.rem(col + step, cols) * auxs + lax.rem(aux + turn, auxs)
                    self.r(index, p, col, aux, 0, False).wait_recv()
            self.r_here(p).wait()

        def c_finish(self, p):
            for step in range(1, count):
                self.c(me, p, lax.rem(me + step, count)).wait_recv()
            self.c_here(me, p).wait()

        def sent(self, p):
            for copy in self.r_own(p):
                copy.wait_send()
            for step in range(1, cols):
                for copy in self.r_pass(p, step)[1]:
                    copy.wait_send()
            for k in range(rows):
                @pl.when(k != me)
                def _(k=k):
                    self.c(k, p, me).wait_send()

                @when(up, row >= k)
                def _(k=k):
                    self.z(k, p, 1).wait_send()

                @when(down, row <= k)
                def _(k=k):
                    self.z(k, p, -1).wait_send()

    b_move = Exchange(b_loc, along_b, brow, bcol, bz_send, bz_recv, bc_send, bc_recv,
                      br_send, br_recv, b_local)
    g_move = Exchange(gown, along_g, grow, gcol, gz_send, gz_recv, gc_send, gc_recv,
                      gr_send, gr_recv, g_local)

    chunks = y.shape[0]
    spare = chunks - 2

    def red_fetch(g, k):
        slot = lax.rem(g, 2)
        return pltpu.make_async_copy(
            amps.at[part(g), pl.ds(k * wide, wide)],
            y.at[spare + slot, pl.ds(k * size, size)],
            red_sem.at[slot, k],
        )

    def tile_rows(t):
        return pl.ds(pl.multiple_of(t * FUSED_ROWS, FUSED_ROWS), FUSED_ROWS)

    def tile_cols(q):
        return pl.ds(pl.multiple_of(q * wide, wide), wide)

    def upd_fetch(q, t):
        return pltpu.make_async_copy(
            amps.at[tile_rows(t), tile_cols(q)], y.at[q, tile_rows(t)], upd_sem.at[q, t]
        )

    def d_copy(p, step, own):
        return pltpu.make_async_remote_copy(
            src_ref=fock.at[part(p)] if own else dcol.at[part(p)],
            dst_ref=dcol.at[part(p)],
            send_sem=d_send.at[(1 - step) // 2, p],
            recv_sem=d_recv.at[p],
            device_id={"row": row + step},
            device_id_type=MESH,
        )

    far_row = jnp.abs(row - me)

    def d_pass(p, step, *conditions):
        @when(row == me, *conditions)
        def _():
            d_copy(p, step, True).start()

        @when(row > me if step > 0 else row < me, *conditions)
        def _():
            d_copy(p, step, False).wait_recv()
            d_copy(p, step, False).start()

    def d_sends(p, *conditions):
        d_pass(p, 1, up, *conditions)
        d_pass(p, -1, down, *conditions)

    def d_finish(p):
        for step, last in ((1, row == rows - 1), (-1, row == 0)):
            @when(row > me if step > 0 else row < me, last)
            def _(step=step):
                d_copy(p, step, False).wait_recv()

    f_load = pltpu.make_async_copy(fock, frow, misc.at[0])
    d_here = pltpu.make_async_copy(fock, dcol, misc.at[1])
    f_load.start()
    for k in range(PIECES):
        red_fetch(0, k).start()
    meet_all(row, col, aux, rows, cols, auxs)

    for p in range(AHEAD):
        b_move.z_own(p)
        b_move.dispatch(row, p, True)

    lane_at = lax.broadcasted_iota(jnp.int32, (1, virt), 1)

    def place(j, held):
        return jnp.where(lane_at == j, eps_virt[virt_at[j]], held)

    virt_row = lax.fori_loop(0, virt, place, jnp.zeros((1, virt), f32), unroll=8)
    spread = jnp.broadcast_to(virt_row, (virt, virt))
    vsum[...] = spread + spread.T

    @pl.loop(0, PIECES)
    def _(p):
        for s in range(1, rows):
            b_move.hop(p, s)

        @pl.when(p + AHEAD < PIECES)
        def _():
            b_move.z_own(p + AHEAD)
            b_move.dispatch(row, p + AHEAD, True)

        b_move.r_start(p)

        @pl.when(p >= 2)
        def _():
            b_move.r_forward(p - 2)

        turn = p - far_row

        @when(turn >= 0, lax.rem(turn, 2) == 0)
        def _():
            for step, inside in ((1, row < rows - 2), (-1, row > 1)):
                d_pass(lax.div(turn, 2), step, inside, turn < 2 * EARLY)

    @pl.when(row == me)
    def _():
        d_here.start()

    @pl.loop(0, EARLY)
    def _(p):
        late = far_row + 2 * p >= PIECES
        d_pass(p, 1, up, jnp.logical_or(row == rows - 2, late))
        d_pass(p, -1, down, jnp.logical_or(row == 1, late))

    @pl.loop(EARLY, PIECES)
    def _(p):
        d_sends(p, row == me)

    for q in range(spare):
        for t in range(tiles):
            upd_fetch(q, t).start()

    @pl.loop(0, PIECES)
    def _(p):
        b_move.c_finish(p)

    def near_copy(g, turn, c):
        other = lax.rem(aux + turn, auxs)
        return pltpu.make_async_remote_copy(
            src_ref=near.at[lax.rem(g, 4), turn - 1, c],
            dst_ref=near_in.at[turn - 1, c, part(g)],
            send_sem=near_send.at[turn - 1, c, g],
            recv_sem=near_recv.at[turn - 1, c, g],
            device_id={"col": col, "aux": other},
            device_id_type=MESH,
        )

    def far_copy(g, step):
        return pltpu.make_async_remote_copy(
            src_ref=far.at[step - 1, part(g)],
            dst_ref=far_in.at[step - 1, part(g)],
            send_sem=far_send.at[step - 1, g],
            recv_sem=far_recv.at[step - 1, g],
            device_id={"col": lax.rem(col + step, cols), "aux": aux},
            device_id_type=MESH,
        )

    def near_sum(g, c):
        total = keep[lax.rem(g, 4), c]
        for turn in range(1, auxs):
            total = total + near_in[turn - 1, c, part(g), :].astype(f32)
        return total

    tile = min(size, 256)
    passes = PIECES // 2

    @pl.loop(0, PIECES + 3)
    def _(j):
        @pl.when(j < PIECES)
        def _():
            @pl.when(j + 1 < PIECES)
            def _():
                for k in range(PIECES):
                    red_fetch(j + 1, k).start()

            for k in range(PIECES):
                red_fetch(j, k).wait()
            slot = lax.rem(j, 4)

            @pl.loop(0, size // tile)
            def _(i):
                rs = pl.ds(pl.multiple_of(i * tile, tile), tile)
                product = jnp.zeros((tile, count * width), f32)
                for k in range(PIECES):
                    at = pl.ds(pl.multiple_of(k * size + i * tile, tile), tile)
                    product = product + jnp.dot(
                        y[spare + lax.rem(j, 2), at, :], bcol[k * wide:(k + 1) * wide, :],
                        preferred_element_type=f32,
                    )

                def slab_of(c, turn):
                    wanted = lax.rem(aux + turn, auxs)
                    value = product[:, c * auxs * width:(c * auxs + 1) * width]
                    for a in range(1, auxs):
                        at = (c * auxs + a) * width
                        value = jnp.where(wanted == a, product[:, at:at + width], value)
                    return value

                for c in range(cols):
                    keep[slot, c, rs, :] = slab_of(c, 0)
                    for turn in range(1, auxs):
                        near[slot, turn - 1, c, rs, :] = slab_of(c, turn).astype(near.dtype)

            for turn in range(1, auxs):
                for c in range(cols):
                    near_copy(j, turn, c).start()

        @when(j >= 1, j <= PIECES)
        def _():
            g = j - 1
            for turn in range(1, auxs):
                for c in range(cols):
                    near_copy(g, turn, c).wait_recv()
            for step in range(1, cols):
                far[step - 1, part(g), :] = near_sum(g, lax.rem(col + step, cols)).astype(far.dtype)
                far_copy(g, step).start()

        @pl.when(j >= 3)
        def _():
            g = j - 3
            total = near_sum(g, col)
            for step in range(1, cols):
                far_copy(g, step).wait_recv()
                total = total + far_in[step - 1, part(g), :].astype(f32)
            gown[part(g), :] = total.astype(gown.dtype)
            for turn in range(1, auxs):
                for c in range(cols):
                    near_copy(g, turn, c).wait_send()

            @pl.when(g < AHEAD)
            def _():
                g_move.z_own(g)

            g_move.r_start(g)

        @when(j >= 3, lax.rem(j, 2) == 1)
        def _():
            p = EARLY + lax.div(j - 3, 2)

            @pl.when(p < PIECES)
            def _():
                d_sends(p, row != me)

        @when(j >= 1, j < 3)
        def _():
            b_move.r_forward(PIECES - 3 + j)

        @when(j >= 3 + passes)
        def _():
            g_move.r_forward(j - 3 - passes)

    g_passed = PIECES - passes
    f_load.wait()
    for q in range(spare, chunks):
        for t in range(tiles):
            upd_fetch(q, t).start()

    @pl.loop(0, PIECES)
    def _(p):
        b_move.r_finish(p)

    def occ_of(block):
        return eps_occ[occ[block * virt]]

    substeps = max(rows - 1, tiles)

    @pl.loop(0, PIECES * substeps)
    def _(n):
        p, t = lax.div(n, substeps), lax.rem(n, substeps)

        @pl.when(t == 0)
        def _():
            g_move.dispatch(row, p, True)

            @pl.when(p + AHEAD < PIECES)
            def _():
                g_move.z_own(p + AHEAD)

        @when(p < LAG, t >= 1)
        def _():
            late = g_passed + p * (substeps - 1) + t - 1

            @pl.when(late < PIECES)
            def _():
                g_move.r_forward(late)

        @pl.when(t + 1 < rows)
        def _():
            g_move.hop(p, t + 1)

        q = p - LAG

        @when(q == 0, t == 0)
        def _():
            @pl.loop(0, PIECES)
            def _(i):
                g_move.r_finish(i)

            @pl.when(row == me)
            def _():
                d_here.wait()

        @when(q >= 0, t < tiles)
        def _():
            @pl.when(t == 0)
            def _():
                g_move.c_finish(q)
                d_finish(q)

            upd_fetch(q, t).wait()
            rs, cs = tile_rows(t), tile_cols(q)
            held = y.at[q, rs]
            acc = residual(
                held, grow[rs, :], brow[rs, :], frow.at[rs],
                gcol[cs, :], bcol[cs, :], dcol.at[cs], virt,
            )
            delta = pair_sums(
                vsum[...], occ_of,
                row * (height // virt) + t * (FUSED_ROWS // virt), FUSED_ROWS,
                me * (across // virt) + q * (wide // virt), wide,
            )
            y[q, rs, :] = (held[...].astype(f32) - acc / delta).astype(y.dtype)

    @pl.loop(PIECES - LAG, PIECES)
    def _(q):
        g_move.c_finish(q)
        d_finish(q)

    @pl.loop(0, PIECES)
    def _(p):
        b_move.sent(p)
        g_move.sent(p)
        for step in range(1, cols):
            far_copy(p, step).wait_send()

        @when(up, row >= me)
        def _():
            d_copy(p, 1, False).wait_send()

        @when(down, row <= me)
        def _():
            d_copy(p, -1, False).wait_send()


def fused(amps, b_loc, fock, occ, virt_at, eps_occ, eps_virt, sizes):
    rows, cols, auxs = sizes
    count = cols * auxs
    height, across = amps.shape
    width, virt = b_loc.shape[1], fock.shape[1]
    full = count * width
    size, wide = height // PIECES, across // PIECES
    tiles = height // FUSED_ROWS
    chunks = PIECES - LAG
    kind = amps.dtype
    any_space = pl.BlockSpec(memory_space=pl.ANY)
    in_smem = pl.BlockSpec(memory_space=pltpu.SMEM)
    in_vmem = pl.BlockSpec(memory_space=pltpu.VMEM)
    hops = (cols - 1) + (auxs - 1) + (cols - 1) * (auxs - 1)
    dma = pltpu.SemaphoreType.DMA
    exchange_sems = [
        dma((2, rows, PIECES)), dma((rows, PIECES)), dma((rows, PIECES)),
        dma((count, PIECES)), dma((hops, PIECES)), dma((count, PIECES)), dma((2, PIECES)),
    ]
    near = max(auxs - 1, 1)
    far = max(cols - 1, 1)

    def shaped(*shape, dtype=kind):
        return jax.ShapeDtypeStruct(shape, dtype)

    return pl.pallas_call(
        functools.partial(fused_kernel, rows, cols, auxs),
        out_shape=(
            pltpu.VMEM((chunks, height, wide), kind),
            pltpu.VMEM((height, full), kind), pltpu.VMEM((height, full), kind),
            pltpu.VMEM((across, full), kind), pltpu.VMEM((across, full), kind),
            pltpu.VMEM((height, virt), kind), pltpu.VMEM((across, virt), kind),
            pltpu.VMEM((virt, virt), jnp.float32),
            shaped(rows, height, width), shaped(rows, height, width),
        ),
        in_specs=[any_space] * 3 + [in_smem] * 4,
        out_specs=(in_vmem,) * 8 + (any_space,) * 2,
        scratch_shapes=[
            pltpu.VMEM((height, width), kind),
            pltpu.VMEM((4, near, cols, size, width), kind),
            pltpu.VMEM((near, cols, height, width), kind),
            pltpu.VMEM((4, cols, size, width), jnp.float32),
            pltpu.VMEM((far, height, width), kind),
            pltpu.VMEM((far, height, width), kind),
            *exchange_sems, *exchange_sems,
            dma((2, PIECES)), dma((PIECES,)),
            dma((near, cols, PIECES)), dma((near, cols, PIECES)),
            dma((far, PIECES)), dma((far, PIECES)),
            dma((2, PIECES)), dma((chunks, tiles)), dma((2,)),
        ],
        compiler_params=pltpu.CompilerParams(
            collective_id=3, has_side_effects=True, vmem_limit_bytes=SCRATCH_BYTES
        ),
        name="fused",
    )(amps, b_loc, fock, occ, virt_at, eps_occ, eps_virt)


def finish_kernel(
    sizes, y, grow, brow, gcol, bcol, frow, dcol, vsum, amps, occ, eps_occ,
    out, held, in_sem, out_sem, move_sem,
):
    cols, auxs = sizes
    row = lax.axis_index("row")
    me = lax.axis_index("col") * auxs + lax.axis_index("aux")
    chunks, height, wide = y.shape
    across = amps.shape[1]
    virt = frow.shape[1]
    tiles = height // FUSED_ROWS
    steps = (across // wide - chunks) * tiles

    def place(n):
        q, t = chunks + lax.div(n, tiles), lax.rem(n, tiles)
        return (
            pl.ds(pl.multiple_of(t * FUSED_ROWS, FUSED_ROWS), FUSED_ROWS),
            pl.ds(pl.multiple_of(q * wide, wide), wide),
        )

    def load(n):
        return pltpu.make_async_copy(amps.at[place(n)], held.at[n], in_sem.at[n])

    def store(n):
        return pltpu.make_async_copy(held.at[n], out.at[place(n)], out_sem.at[n])

    def move(q):
        return pltpu.make_async_copy(
            y.at[q], out.at[:, pl.ds(q * wide, wide)], move_sem.at[q]
        )

    for n in range(steps):
        load(n).start()
    for q in range(chunks):
        move(q).start()

    def occ_of(block):
        return eps_occ[occ[block * virt]]

    @pl.loop(0, steps)
    def _(n):
        q, t = chunks + lax.div(n, tiles), lax.rem(n, tiles)
        rs, cs = place(n)
        load(n).wait()
        tile = held.at[n]
        acc = residual(
            tile, grow[rs, :], brow[rs, :], frow.at[rs],
            gcol[cs, :], bcol[cs, :], dcol.at[cs], virt,
        )
        delta = pair_sums(
            vsum[...], occ_of,
            row * (height // virt) + t * (FUSED_ROWS // virt), FUSED_ROWS,
            me * (across // virt) + q * (wide // virt), wide,
        )
        held[n] = (tile[...].astype(jnp.float32) - acc / delta).astype(held.dtype)
        store(n).start()

    for n in range(steps):
        store(n).wait()
    for q in range(chunks):
        move(q).wait()


def finish(y, kept, amps, occ, eps_occ, sizes):
    chunks, height, wide = y.shape
    steps = (amps.shape[1] // wide - chunks) * (height // FUSED_ROWS)
    here = [pltpu.with_memory_space_constraint(x, pltpu.VMEM) for x in (y, *kept)]
    any_space = pl.BlockSpec(memory_space=pl.ANY)
    in_smem = pl.BlockSpec(memory_space=pltpu.SMEM)
    in_vmem = pl.BlockSpec(memory_space=pltpu.VMEM)
    return pl.pallas_call(
        functools.partial(finish_kernel, sizes[1:]),
        out_shape=jax.ShapeDtypeStruct(amps.shape, amps.dtype),
        in_specs=[in_vmem] * len(here) + [any_space, in_smem, in_smem],
        out_specs=any_space,
        scratch_shapes=[
            pltpu.VMEM((steps, FUSED_ROWS, wide), amps.dtype),
            pltpu.SemaphoreType.DMA((steps,)),
            pltpu.SemaphoreType.DMA((steps,)),
            pltpu.SemaphoreType.DMA((chunks,)),
        ],
        compiler_params=pltpu.CompilerParams(vmem_limit_bytes=SCRATCH_BYTES),
        name="finish",
    )(*here, amps, occ, eps_occ)


def fits(sizes, height, across, width, virt):
    rows, cols, auxs = sizes
    return (
        rows == cols * auxs
        and width % LANES == 0
        and height % (4 * FUSED_ROWS) == 0
        and across % (PIECES * virt) == 0
        and rows > 1 and cols > 1 and auxs > 1
    )


def body(sizes, amplitudes, b_factors, fock_blocks, occ_index, virt_index, eps_occ, eps_virt):
    height, across = amplitudes.shape
    if not fits(sizes, height, across, b_factors.shape[1], fock_blocks.shape[1]):
        return staged_body(
            sizes, amplitudes, b_factors, fock_blocks, occ_index, virt_index, eps_occ, eps_virt
        )
    y, *kept, _, _ = fused(
        amplitudes, b_factors, fock_blocks, occ_index, virt_index, eps_occ, eps_virt, sizes
    )
    return finish(y, kept, amplitudes, occ_index, eps_occ, sizes)


def solution(mesh):
    in_specs = (
        P(("groups", "row"), ("col", "aux")),
        P(("groups", "row"), ("col", "aux")),
        P(("groups", "row"), None),
        P("groups"),
        P("groups"),
        P("groups"),
        P("groups"),
    )
    out_specs = P(("groups", "row"), ("col", "aux"))
    sizes = (mesh.shape["row"], mesh.shape["col"], mesh.shape["aux"])
    return jax.shard_map(
        functools.partial(body, sizes),
        mesh=mesh, in_specs=in_specs, out_specs=out_specs, check_vma=False,
    )
```

```python
import functools

import jax
import jax.numpy as jnp
from jax import lax
from jax.experimental import pallas as pl
from jax.experimental.pallas import tpu as pltpu
from jax.sharding import PartitionSpec as P

MESH = pl.DeviceIdType.MESH
LANES = 128
ROW_TILE = 512
COL_TILE = 1024
VMEM_BYTES = 60 * 1024 * 1024


def pair_energy(occ_part, virt_part, eps_occ, eps_virt):
    virt_hit = virt_part[:, None] == jnp.arange(eps_virt.shape[0], dtype=jnp.int32)[None, :]
    occ_hit = occ_part[:, None] == jnp.arange(eps_occ.shape[0], dtype=jnp.int32)[None, :]
    upper = jnp.sum(jnp.where(virt_hit, eps_virt[None, :], 0.0), axis=1)
    lower = jnp.sum(jnp.where(occ_hit, eps_occ[None, :], 0.0), axis=1)
    return upper - lower


def slab(ref, index, width, start, size):
    if width % LANES == 0:
        return ref.at[pl.ds(start, size), pl.ds(pl.multiple_of(index * width, LANES), width)]
    return ref.at[index, pl.ds(start, size)]


def slab_shape(count, rows, width):
    return (rows, count * width) if width % LANES == 0 else (count, rows, width)


def whole(array):
    if array.ndim == 2:
        return array
    count, rows, width = array.shape
    return array.transpose(1, 0, 2).reshape(rows, count * width)


def meet(row, col, aux, rows, cols, auxs):
    barrier = pltpu.get_barrier_semaphore()

    def greet(device):
        pl.semaphore_signal(barrier, inc=1, device_id=device, device_id_type=MESH)

    @pl.when(row > 0)
    def _():
        greet({"row": row - 1})

    @pl.when(row < rows - 1)
    def _():
        greet({"row": row + 1})

    for step in range(1, cols * auxs):
        other = lax.rem(col * auxs + aux + step, cols * auxs)
        greet({"col": other // auxs, "aux": lax.rem(other, auxs)})
    above = jnp.where(row > 0, 1, 0)
    below = jnp.where(row < rows - 1, 1, 0)
    pl.semaphore_wait(barrier, cols * auxs - 1 + above + below)


def exchange_kernel(
    rows, cols, auxs, pieces, loc, along, mine, other,
    zsend, zrecv, csend, crecv, rsend, rrecv, lsem,
):
    row, col, aux = lax.axis_index("row"), lax.axis_index("col"), lax.axis_index("aux")
    count = cols * auxs
    me = col * auxs + aux
    height, width = loc.shape
    size = height // pieces
    meet(row, col, aux, rows, cols, auxs)

    def held(k, p, own):
        return loc.at[pl.ds(p * size, size)] if own else along.at[k, pl.ds(p * size, size)]

    def z_copy(k, p, step, own=False):
        return pltpu.make_async_remote_copy(
            src_ref=held(k, p, own),
            dst_ref=along.at[k, pl.ds(p * size, size)],
            send_sem=zsend.at[(1 - step) // 2, k, p],
            recv_sem=zrecv.at[k, p],
            device_id={"row": row + step},
            device_id_type=MESH,
        )

    def c_copy(k, p, slot, own=False):
        return pltpu.make_async_remote_copy(
            src_ref=held(k, p, own),
            dst_ref=slab(other, slot, width, p * size, size),
            send_sem=csend.at[k, p],
            recv_sem=crecv.at[slot, p],
            device_id={"col": k // auxs, "aux": lax.rem(k, auxs)},
            device_id_type=MESH,
        )

    def c_local(k, p, own=False):
        return pltpu.make_async_copy(
            held(k, p, own), slab(other, me, width, p * size, size), lsem.at[1 + p]
        )

    def dispatch(k, p, own=False):
        @pl.when(k != me)
        def _():
            c_copy(k, p, me, own).start()

        @pl.when(k == me)
        def _():
            c_local(k, p, own).start()

    def r_copy(index, to_col, to_aux, hop, own):
        return pltpu.make_async_remote_copy(
            src_ref=loc if own else slab(mine, index, width, 0, height),
            dst_ref=slab(mine, index, width, 0, height),
            send_sem=rsend.at[hop],
            recv_sem=rrecv.at[index],
            device_id={"col": to_col, "aux": to_aux},
            device_id_type=MESH,
        )

    def r_sends():
        first, second = [], []
        for step in range(1, cols):
            first.append(r_copy(me, lax.rem(col + step, cols), aux, step - 1, True))
        hop = cols - 1
        for step in range(cols):
            from_col = lax.rem(col + step, cols)
            for turn in range(1, auxs):
                second.append((
                    from_col * auxs + aux,
                    r_copy(from_col * auxs + aux, col, lax.rem(aux + turn, auxs), hop, step == 0),
                ))
                hop += 1
        return first, second

    first, second = r_sends()
    for copy in first:
        copy.start()
    for _, copy in second[: auxs - 1]:
        copy.start()
    for p in range(pieces):
        @pl.when(row < rows - 1)
        def _(p=p):
            z_copy(row, p, 1, True).start()

        @pl.when(row > 0)
        def _(p=p):
            z_copy(row, p, -1, True).start()

        dispatch(row, p, True)
    local = pltpu.make_async_copy(loc, slab(mine, me, width, 0, height), lsem.at[0])
    local.start()

    for s in range(1, rows):
        for p in range(pieces):
            @pl.when(row - s >= 0)
            def _(s=s, p=p):
                k = row - s
                z_copy(k, p, 1).wait_recv()

                @pl.when(row < rows - 1)
                def _():
                    z_copy(k, p, 1).start()

                dispatch(k, p)

            @pl.when(row + s < rows)
            def _(s=s, p=p):
                k = row + s
                z_copy(k, p, -1).wait_recv()

                @pl.when(row > 0)
                def _():
                    z_copy(k, p, -1).start()

                dispatch(k, p)
        if s == max(1, rows - 2):
            for index, copy in second[auxs - 1:]:
                r_copy(index, col, aux, 0, False).wait_recv()
                copy.start()

    for step in range(cols):
        from_col = lax.rem(col + step, cols)
        for turn in range(1, auxs):
            index = from_col * auxs + lax.rem(aux + turn, auxs)
            r_copy(index, col, aux, 0, False).wait_recv()
    for copy in first:
        copy.wait_send()
    for _, copy in second:
        copy.wait_send()
    local.wait()
    for step in range(1, count):
        index = lax.rem(me + step, count)
        for p in range(pieces):
            c_copy(me, p, index).wait_recv()
    for k in range(rows):
        for p in range(pieces):
            @pl.when(k != me)
            def _(k=k, p=p):
                c_copy(k, p, me).wait_send()

            @pl.when(k == me)
            def _(k=k, p=p):
                c_local(k, p).wait()

            @pl.when((row < rows - 1) & (row >= k))
            def _(k=k, p=p):
                z_copy(k, p, 1).wait_send()

            @pl.when((row > 0) & (row <= k))
            def _(k=k, p=p):
                z_copy(k, p, -1).wait_send()


def exchange(loc, sizes, collective_id):
    rows, cols, auxs = sizes
    count = cols * auxs
    height, width = loc.shape
    pieces = max(1, 32 // rows)
    shape = slab_shape(count, height, width)
    hops = cols - 1 + cols * (auxs - 1)
    any_space = pl.BlockSpec(memory_space=pl.ANY)
    _, mine, other = pl.pallas_call(
        functools.partial(exchange_kernel, rows, cols, auxs, pieces),
        out_shape=(
            jax.ShapeDtypeStruct((rows, height, width), loc.dtype),
            jax.ShapeDtypeStruct(shape, loc.dtype),
            jax.ShapeDtypeStruct(shape, loc.dtype),
        ),
        in_specs=[any_space],
        out_specs=(any_space, any_space, any_space),
        scratch_shapes=[
            pltpu.SemaphoreType.DMA((2, rows, pieces)),
            pltpu.SemaphoreType.DMA((rows, pieces)),
            pltpu.SemaphoreType.DMA((rows, pieces)),
            pltpu.SemaphoreType.DMA((count, pieces)),
            pltpu.SemaphoreType.DMA((hops,)),
            pltpu.SemaphoreType.DMA((count,)),
            pltpu.SemaphoreType.DMA((1 + pieces,)),
        ],
        compiler_params=pltpu.CompilerParams(
            collective_id=collective_id, has_side_effects=True
        ),
        name="exchange%d" % collective_id,
    )(loc)
    return whole(mine), whole(other)


def reduce_kernel(
    rows, cols, auxs, groups, amps, b_col, fock, total, diag, part, landed, held,
    psend, precv, dsend, drecv, lsem, tsem,
):
    row, col, aux = lax.axis_index("row"), lax.axis_index("col"), lax.axis_index("aux")
    count = cols * auxs
    me = col * auxs + aux
    height, width = total.shape
    size = height // groups
    tile = min(size, 256)

    def fetch(g):
        return pltpu.make_async_copy(
            amps.at[pl.ds(g * size, size)], held.at[g % 2], tsem.at[g % 2]
        )

    fetch(0).start()
    meet(row, col, aux, rows, cols, auxs)

    def p_copy(g, index, slot):
        return pltpu.make_async_remote_copy(
            src_ref=part.at[index, pl.ds(g * size, size)],
            dst_ref=landed.at[slot, pl.ds(g * size, size)],
            send_sem=psend.at[g, index],
            recv_sem=precv.at[g, slot],
            device_id={"col": index // auxs, "aux": lax.rem(index, auxs)},
            device_id_type=MESH,
        )

    def d_copy(p, step, own):
        piece = pl.ds(p * size, size)
        return pltpu.make_async_remote_copy(
            src_ref=fock.at[piece] if own else diag.at[piece],
            dst_ref=diag.at[piece],
            send_sem=dsend.at[(1 - step) // 2, p],
            recv_sem=drecv.at[p],
            device_id={"row": row + step},
            device_id_type=MESH,
        )

    own_diag = pltpu.make_async_copy(fock, diag, lsem.at[0])
    up, down = row < rows - 1, row > 0

    @pl.when(row == me)
    def _():
        own_diag.start()

    for p in range(groups):
        @pl.when((row == me) & up)
        def _(p=p):
            d_copy(p, 1, True).start()

        @pl.when((row == me) & down)
        def _(p=p):
            d_copy(p, -1, True).start()

    def forward(p):
        @pl.when(row > me)
        def _():
            d_copy(p, 1, False).wait_recv()

            @pl.when(up)
            def _():
                d_copy(p, 1, False).start()

        @pl.when(row < me)
        def _():
            d_copy(p, -1, False).wait_recv()

            @pl.when(down)
            def _():
                d_copy(p, -1, False).start()

    ahead = max(groups // 2, 1)
    for g in range(groups):
        if g + 1 < groups:
            fetch(g + 1).start()
        fetch(g).wait()

        @pl.loop(0, size // tile)
        def _(i, g=g):
            at = pl.ds(pl.multiple_of(i * tile, tile), tile)
            to = pl.ds(pl.multiple_of(g * size + i * tile, tile), tile)
            product = jnp.dot(
                held[g % 2, at, :], b_col[...], preferred_element_type=jnp.float32
            ).astype(part.dtype)
            for index in range(count):
                part[index, to, :] = product[:, index * width:(index + 1) * width]

        for step in range(1, count):
            p_copy(g, lax.rem(me + step, count), me).start()
        if g >= ahead:
            forward(g - ahead)
    for p in range(groups - ahead, groups):
        forward(p)

    for g in range(groups):
        for step in range(1, count):
            p_copy(g, me, lax.rem(me + step, count)).wait_recv()

        @pl.loop(0, size // tile)
        def _(i, g=g):
            at = pl.ds(pl.multiple_of(g * size + i * tile, tile), tile)
            acc = part[me, at, :].astype(jnp.float32)
            for step in range(1, count):
                index = lax.rem(me + step, count)
                acc = acc + landed[index, at, :].astype(jnp.float32)
            total[at, :] = acc.astype(total.dtype)

    for g in range(groups):
        for step in range(1, count):
            p_copy(g, lax.rem(me + step, count), me).wait_send()

    @pl.when(row == me)
    def _():
        own_diag.wait()

    for p in range(groups):
        @pl.when(up & (row >= me))
        def _(p=p):
            d_copy(p, 1, False).wait_send()

        @pl.when(down & (row <= me))
        def _(p=p):
            d_copy(p, -1, False).wait_send()


def reduce_rows(amps, b_cols, fock, sizes, collective_id):
    rows, cols, auxs = sizes
    count = cols * auxs
    height, virt = fock.shape
    across = amps.shape[1]
    width = b_cols.shape[1] // count
    groups = max(1, height // 512)
    any_space = pl.BlockSpec(memory_space=pl.ANY)
    in_vmem = pl.BlockSpec(memory_space=pltpu.VMEM)
    return pl.pallas_call(
        functools.partial(reduce_kernel, rows, cols, auxs, groups),
        out_shape=(
            jax.ShapeDtypeStruct((height, width), amps.dtype),
            jax.ShapeDtypeStruct((height, virt), fock.dtype),
        ),
        in_specs=[any_space, in_vmem, any_space],
        out_specs=(in_vmem, any_space),
        scratch_shapes=[
            pltpu.VMEM((count, height, width), amps.dtype),
            pltpu.VMEM((count, height, width), amps.dtype),
            pltpu.VMEM((2, height // groups, across), amps.dtype),
            pltpu.SemaphoreType.DMA((groups, count)),
            pltpu.SemaphoreType.DMA((groups, count)),
            pltpu.SemaphoreType.DMA((2, groups)),
            pltpu.SemaphoreType.DMA((groups,)),
            pltpu.SemaphoreType.DMA((1,)),
            pltpu.SemaphoreType.DMA((2,)),
        ],
        compiler_params=pltpu.CompilerParams(
            collective_id=collective_id, has_side_effects=True, vmem_limit_bytes=VMEM_BYTES
        ),
        name="reduce%d" % collective_id,
    )(amps, b_cols, fock)


def update_kernel(
    virt, tile, t_ref, g_row, b_row, f_row, e_row, g_col, b_col, f_col, e_col, out
):
    high, across = t_ref.shape
    contract = (((1,), (1,)), ((), ()))

    @pl.loop(0, across // tile)
    def _(j):
        base = pl.multiple_of(j * tile, tile)
        at = pl.ds(base, tile)
        acc = lax.dot_general(
            g_row[...], b_col[at, :], contract, preferred_element_type=jnp.float32
        )
        acc = acc + lax.dot_general(
            b_row[...], g_col[at, :], contract, preferred_element_type=jnp.float32
        )
        right = [
            jnp.dot(
                t_ref[:, pl.ds(pl.multiple_of(base + k * virt, virt), virt)],
                f_col[pl.ds(pl.multiple_of(base + k * virt, virt), virt), :],
                preferred_element_type=jnp.float32,
            )
            for k in range(tile // virt)
        ]
        left = [
            lax.dot_general(
                f_row[k * virt:(k + 1) * virt, :],
                t_ref[k * virt:(k + 1) * virt, at],
                (((0,), (0,)), ((), ())),
                preferred_element_type=jnp.float32,
            )
            for k in range(high // virt)
        ]
        acc = acc + jnp.concatenate(right, axis=1) + jnp.concatenate(left, axis=0)
        delta = e_row[...] + e_col[:, at]
        out[:, at] = (t_ref[:, at].astype(jnp.float32) - acc / delta).astype(out.dtype)


def update(amplitudes, g_rows, b_rows, fock, e_rows, g_cols, b_cols, diag, e_cols):
    high, across = amplitudes.shape
    virt = fock.shape[1]
    aux = b_rows.shape[1]
    row_tile, col_tile = min(ROW_TILE, high), min(COL_TILE, across)
    by_row = lambda i: (i, 0)
    fixed = lambda i: (0, 0)
    return pl.pallas_call(
        functools.partial(update_kernel, virt, col_tile),
        out_shape=jax.ShapeDtypeStruct(amplitudes.shape, amplitudes.dtype),
        grid=(high // row_tile,),
        in_specs=[
            pl.BlockSpec((row_tile, across), by_row),
            pl.BlockSpec((row_tile, aux), by_row),
            pl.BlockSpec((row_tile, aux), by_row),
            pl.BlockSpec((row_tile, virt), by_row),
            pl.BlockSpec((row_tile, 1), by_row),
            pl.BlockSpec((across, aux), fixed),
            pl.BlockSpec((across, aux), fixed),
            pl.BlockSpec((across, virt), fixed),
            pl.BlockSpec((1, across), fixed),
        ],
        out_specs=pl.BlockSpec((row_tile, across), by_row),
        compiler_params=pltpu.CompilerParams(vmem_limit_bytes=VMEM_BYTES),
        name="update",
    )(amplitudes, g_rows, b_rows, fock, e_rows, g_cols, b_cols, diag, e_cols)


def staged_body(sizes, amplitudes, b_factors, fock_blocks, occ_index, virt_index, eps_occ, eps_virt):
    height, across = amplitudes.shape
    b_rows, b_cols = exchange(b_factors, sizes, 0)
    g_own, diag = reduce_rows(amplitudes, b_cols, fock_blocks, sizes, 1)
    g_rows, g_cols = exchange(g_own, sizes, 2)

    def energy(start, size):
        return pair_energy(
            lax.dynamic_slice_in_dim(occ_index, start, size),
            lax.dynamic_slice_in_dim(virt_index, start, size),
            eps_occ,
            eps_virt,
        )

    e_rows = energy(lax.axis_index("row") * height, height)
    e_cols = energy(lax.axis_index(("col", "aux")) * across, across)
    return update(
        amplitudes, g_rows, b_rows, fock_blocks, e_rows[:, None],
        g_cols, b_cols, diag, e_cols[None, :],
    )


PIECES = 8
LAG = 2
AHEAD = 4
EARLY = PIECES // 2
FUSED_ROWS = 1024
SCRATCH_BYTES = 19 * 1024 * 1024
NT = (((1,), (1,)), ((), ()))
TN = (((0,), (0,)), ((), ()))


def when(*conditions):
    flag = conditions[0]
    for condition in conditions[1:]:
        flag = jnp.logical_and(flag, condition)
    return pl.when(flag)


def residual(t, g_row, b_row, f_row, g_col, b_col, f_col, virt):
    f32 = jnp.float32
    high, wide = t.shape
    acc = lax.dot_general(g_row, b_col, NT, preferred_element_type=f32)
    acc = acc + lax.dot_general(b_row, g_col, NT, preferred_element_type=f32)
    right = [
        jnp.dot(
            t[:, k * virt:(k + 1) * virt], f_col[k * virt:(k + 1) * virt, :],
            preferred_element_type=f32,
        )
        for k in range(wide // virt)
    ]
    left = [
        lax.dot_general(
            f_row[k * virt:(k + 1) * virt, :], t[k * virt:(k + 1) * virt, :], TN,
            preferred_element_type=f32,
        )
        for k in range(high // virt)
    ]
    return acc + jnp.concatenate(right, axis=1) + jnp.concatenate(left, axis=0)


def pair_sums(virt_sum, occ_of, row_block, high, col_block, wide):
    virt = virt_sum.shape[0]
    return jnp.concatenate([
        jnp.concatenate([
            virt_sum - (occ_of(row_block + a) + occ_of(col_block + c))
            for c in range(wide // virt)
        ], axis=1)
        for a in range(high // virt)
    ], axis=0)


def meet_all(row, col, aux, rows, cols, auxs):
    barrier = pltpu.get_barrier_semaphore()
    for step in range(1, rows):
        pl.semaphore_signal(
            barrier, inc=1, device_id={"row": lax.rem(row + step, rows)}, device_id_type=MESH
        )
    for step in range(1, cols * auxs):
        other = lax.rem(col * auxs + aux + step, cols * auxs)
        pl.semaphore_signal(
            barrier, inc=1, device_id={"col": other // auxs, "aux": lax.rem(other, auxs)},
            device_id_type=MESH,
        )
    pl.semaphore_wait(barrier, rows + cols * auxs - 2)


def fused_kernel(
    rows, cols, auxs,
    amps, b_loc, fock, occ, virt_at, eps_occ, eps_virt,
    y, grow, brow, gcol, bcol, frow, dcol, vsum, along_b, along_g,
    gown, near, near_in, keep, far, far_in,
    bz_send, bz_recv, bc_send, bc_recv, br_send, br_recv, b_local,
    gz_send, gz_recv, gc_send, gc_recv, gr_send, gr_recv, g_local,
    d_send, d_recv, near_send, near_recv, far_send, far_recv,
    red_sem, upd_sem, misc,
):
    row, col, aux = lax.axis_index("row"), lax.axis_index("col"), lax.axis_index("aux")
    count = cols * auxs
    me = col * auxs + aux
    height, width = b_loc.shape
    across = amps.shape[1]
    virt = fock.shape[1]
    size = height // PIECES
    wide = across // PIECES
    tiles = height // FUSED_ROWS
    up, down = row < rows - 1, row > 0
    f32 = jnp.float32

    def part(p):
        return pl.ds(pl.multiple_of(p * size, size), size)

    def at_core(index):
        return {"col": lax.div(index, auxs), "aux": lax.rem(index, auxs)}

    class Exchange:
        def __init__(self, loc, along, mine, other, z_send, z_recv, c_send, c_recv,
                     r_send, r_recv, local):
            self.loc, self.along, self.mine, self.other = loc, along, mine, other
            self.z_send, self.z_recv = z_send, z_recv
            self.c_send, self.c_recv = c_send, c_recv
            self.r_send, self.r_recv, self.local = r_send, r_recv, local

        def held(self, k, p, own):
            return self.loc.at[part(p)] if own else self.along.at[k, part(p)]

        def lane(self, ref, index, p):
            return ref.at[part(p), pl.ds(pl.multiple_of(index * width, LANES), width)]

        def z(self, k, p, step, own=False):
            return pltpu.make_async_remote_copy(
                src_ref=self.held(k, p, own),
                dst_ref=self.along.at[k, part(p)],
                send_sem=self.z_send.at[(1 - step) // 2, k, p],
                recv_sem=self.z_recv.at[k, p],
                device_id={"row": row + step},
                device_id_type=MESH,
            )

        def z_own(self, p):
            @pl.when(up)
            def _():
                self.z(row, p, 1, True).start()

            @pl.when(down)
            def _():
                self.z(row, p, -1, True).start()

        def c(self, k, p, slot, own=False):
            return pltpu.make_async_remote_copy(
                src_ref=self.held(k, p, own),
                dst_ref=self.lane(self.other, slot, p),
                send_sem=self.c_send.at[k, p],
                recv_sem=self.c_recv.at[slot, p],
                device_id=at_core(k),
                device_id_type=MESH,
            )

        def c_here(self, k, p, own=False):
            return pltpu.make_async_copy(
                self.held(k, p, own), self.lane(self.other, me, p), self.local.at[1, p]
            )

        def dispatch(self, k, p, own=False):
            @pl.when(k != me)
            def _():
                self.c(k, p, me, own).start()

            @pl.when(k == me)
            def _():
                self.c_here(k, p, own).start()

        def hop(self, p, s):
            @pl.when(row - s >= 0)
            def _():
                k = row - s
                self.z(k, p, 1).wait_recv()

                @pl.when(up)
                def _():
                    self.z(k, p, 1).start()

                self.dispatch(k, p)

            @pl.when(row + s < rows)
            def _():
                k = row + s
                self.z(k, p, -1).wait_recv()

                @pl.when(down)
                def _():
                    self.z(k, p, -1).start()

                self.dispatch(k, p)

        def r(self, index, p, to_col, to_aux, hop, own):
            return pltpu.make_async_remote_copy(
                src_ref=self.loc.at[part(p)] if own else self.lane(self.mine, index, p),
                dst_ref=self.lane(self.mine, index, p),
                send_sem=self.r_send.at[hop, p],
                recv_sem=self.r_recv.at[index, p],
                device_id={"col": to_col, "aux": to_aux},
                device_id_type=MESH,
            )

        def r_here(self, p):
            return pltpu.make_async_copy(
                self.loc.at[part(p)], self.lane(self.mine, me, p), self.local.at[0, p]
            )

        def r_own(self, p):
            copies = [
                self.r(me, p, lax.rem(col + step, cols), aux, step - 1, True)
                for step in range(1, cols)
            ]
            for turn in range(1, auxs):
                copies.append(
                    self.r(me, p, col, lax.rem(aux + turn, auxs), cols - 2 + turn, True)
                )
            return copies

        def r_start(self, p):
            for copy in self.r_own(p):
                copy.start()
            self.r_here(p).start()

        def r_pass(self, p, step):
            index = lax.rem(col + step, cols) * auxs + aux
            base = cols - 1 + auxs - 1 + (step - 1) * (auxs - 1)
            return index, [
                self.r(index, p, col, lax.rem(aux + turn, auxs), base + turn - 1, False)
                for turn in range(1, auxs)
            ]

        def r_forward(self, p):
            for step in range(1, cols):
                index, copies = self.r_pass(p, step)
                self.r(index, p, col, aux, 0, False).wait_recv()
                for copy in copies:
                    copy.start()

        def r_finish(self, p):
            for step in range(cols):
                for turn in range(1, auxs):
                    index = lax.rem(col + step, cols) * auxs + lax.rem(aux + turn, auxs)
                    self.r(index, p, col, aux, 0, False).wait_recv()
            self.r_here(p).wait()

        def c_finish(self, p):
            for step in range(1, count):
                self.c(me, p, lax.rem(me + step, count)).wait_recv()
            self.c_here(me, p).wait()

        def sent(self, p):
            for copy in self.r_own(p):
                copy.wait_send()
            for step in range(1, cols):
                for copy in self.r_pass(p, step)[1]:
                    copy.wait_send()
            for k in range(rows):
                @pl.when(k != me)
                def _(k=k):
                    self.c(k, p, me).wait_send()

                @when(up, row >= k)
                def _(k=k):
                    self.z(k, p, 1).wait_send()

                @when(down, row <= k)
                def _(k=k):
                    self.z(k, p, -1).wait_send()

    b_move = Exchange(b_loc, along_b, brow, bcol, bz_send, bz_recv, bc_send, bc_recv,
                      br_send, br_recv, b_local)
    g_move = Exchange(gown, along_g, grow, gcol, gz_send, gz_recv, gc_send, gc_recv,
                      gr_send, gr_recv, g_local)

    chunks = y.shape[0]
    spare = chunks - 2

    def red_fetch(g, k):
        slot = lax.rem(g, 2)
        return pltpu.make_async_copy(
            amps.at[part(g), pl.ds(k * wide, wide)],
            y.at[spare + slot, pl.ds(k * size, size)],
            red_sem.at[slot, k],
        )

    def tile_rows(t):
        return pl.ds(pl.multiple_of(t * FUSED_ROWS, FUSED_ROWS), FUSED_ROWS)

    def tile_cols(q):
        return pl.ds(pl.multiple_of(q * wide, wide), wide)

    def upd_fetch(q, t):
        return pltpu.make_async_copy(
            amps.at[tile_rows(t), tile_cols(q)], y.at[q, tile_rows(t)], upd_sem.at[q, t]
        )

    def d_copy(p, step, own):
        return pltpu.make_async_remote_copy(
            src_ref=fock.at[part(p)] if own else dcol.at[part(p)],
            dst_ref=dcol.at[part(p)],
            send_sem=d_send.at[(1 - step) // 2, p],
            recv_sem=d_recv.at[p],
            device_id={"row": row + step},
            device_id_type=MESH,
        )

    far_row = jnp.abs(row - me)

    def d_pass(p, step, *conditions):
        @when(row == me, *conditions)
        def _():
            d_copy(p, step, True).start()

        @when(row > me if step > 0 else row < me, *conditions)
        def _():
            d_copy(p, step, False).wait_recv()
            d_copy(p, step, False).start()

    def d_sends(p, *conditions):
        d_pass(p, 1, up, *conditions)
        d_pass(p, -1, down, *conditions)

    def d_finish(p):
        for step, last in ((1, row == rows - 1), (-1, row == 0)):
            @when(row > me if step > 0 else row < me, last)
            def _(step=step):
                d_copy(p, step, False).wait_recv()

    f_load = pltpu.make_async_copy(fock, frow, misc.at[0])
    d_here = pltpu.make_async_copy(fock, dcol, misc.at[1])
    f_load.start()
    for k in range(PIECES):
        red_fetch(0, k).start()
    meet_all(row, col, aux, rows, cols, auxs)

    for p in range(AHEAD):
        b_move.z_own(p)
        b_move.dispatch(row, p, True)

    lane_at = lax.broadcasted_iota(jnp.int32, (1, virt), 1)

    def place(j, held):
        return jnp.where(lane_at == j, eps_virt[virt_at[j]], held)

    virt_row = lax.fori_loop(0, virt, place, jnp.zeros((1, virt), f32), unroll=8)
    spread = jnp.broadcast_to(virt_row, (virt, virt))
    vsum[...] = spread + spread.T

    @pl.loop(0, PIECES)
    def _(p):
        for s in range(1, rows):
            b_move.hop(p, s)

        @pl.when(p + AHEAD < PIECES)
        def _():
            b_move.z_own(p + AHEAD)
            b_move.dispatch(row, p + AHEAD, True)

        b_move.r_start(p)

        @pl.when(p >= 2)
        def _():
            b_move.r_forward(p - 2)

        turn = p - far_row

        @when(turn >= 0, lax.rem(turn, 2) == 0)
        def _():
            for step, inside in ((1, row < rows - 2), (-1, row > 1)):
                d_pass(lax.div(turn, 2), step, inside, turn < 2 * EARLY)

    @pl.when(row == me)
    def _():
        d_here.start()

    @pl.loop(0, EARLY)
    def _(p):
        late = far_row + 2 * p >= PIECES
        d_pass(p, 1, up, jnp.logical_or(row == rows - 2, late))
        d_pass(p, -1, down, jnp.logical_or(row == 1, late))

    @pl.loop(EARLY, PIECES)
    def _(p):
        d_sends(p, row == me)

    for q in range(spare):
        for t in range(tiles):
            upd_fetch(q, t).start()

    @pl.loop(0, PIECES)
    def _(p):
        b_move.c_finish(p)

    def near_copy(g, turn, c):
        other = lax.rem(aux + turn, auxs)
        return pltpu.make_async_remote_copy(
            src_ref=near.at[lax.rem(g, 4), turn - 1, c],
            dst_ref=near_in.at[turn - 1, c, part(g)],
            send_sem=near_send.at[turn - 1, c, g],
            recv_sem=near_recv.at[turn - 1, c, g],
            device_id={"col": col, "aux": other},
            device_id_type=MESH,
        )

    def far_copy(g, step):
        return pltpu.make_async_remote_copy(
            src_ref=far.at[step - 1, part(g)],
            dst_ref=far_in.at[step - 1, part(g)],
            send_sem=far_send.at[step - 1, g],
            recv_sem=far_recv.at[step - 1, g],
            device_id={"col": lax.rem(col + step, cols), "aux": aux},
            device_id_type=MESH,
        )

    def near_sum(g, c):
        total = keep[lax.rem(g, 4), c]
        for turn in range(1, auxs):
            total = total + near_in[turn - 1, c, part(g), :].astype(f32)
        return total

    tile = min(size, 256)
    passes = PIECES // 2

    @pl.loop(0, PIECES + 3)
    def _(j):
        @pl.when(j < PIECES)
        def _():
            @pl.when(j + 1 < PIECES)
            def _():
                for k in range(PIECES):
                    red_fetch(j + 1, k).start()

            for k in range(PIECES):
                red_fetch(j, k).wait()
            slot = lax.rem(j, 4)

            @pl.loop(0, size // tile)
            def _(i):
                rs = pl.ds(pl.multiple_of(i * tile, tile), tile)
                product = jnp.zeros((tile, count * width), f32)
                for k in range(PIECES):
                    at = pl.ds(pl.multiple_of(k * size + i * tile, tile), tile)
                    product = product + jnp.dot(
                        y[spare + lax.rem(j, 2), at, :], bcol[k * wide:(k + 1) * wide, :],
                        preferred_element_type=f32,
                    )

                def slab_of(c, turn):
                    wanted = lax.rem(aux + turn, auxs)
                    value = product[:, c * auxs * width:(c * auxs + 1) * width]
                    for a in range(1, auxs):
                        at = (c * auxs + a) * width
                        value = jnp.where(wanted == a, product[:, at:at + width], value)
                    return value

                for c in range(cols):
                    keep[slot, c, rs, :] = slab_of(c, 0)
                    for turn in range(1, auxs):
                        near[slot, turn - 1, c, rs, :] = slab_of(c, turn).astype(near.dtype)

            for turn in range(1, auxs):
                for c in range(cols):
                    near_copy(j, turn, c).start()

        @when(j >= 1, j <= PIECES)
        def _():
            g = j - 1
            for turn in range(1, auxs):
                for c in range(cols):
                    near_copy(g, turn, c).wait_recv()
            for step in range(1, cols):
                far[step - 1, part(g), :] = near_sum(g, lax.rem(col + step, cols)).astype(far.dtype)
                far_copy(g, step).start()

        @pl.when(j >= 3)
        def _():
            g = j - 3
            total = near_sum(g, col)
            for step in range(1, cols):
                far_copy(g, step).wait_recv()
                total = total + far_in[step - 1, part(g), :].astype(f32)
            gown[part(g), :] = total.astype(gown.dtype)
            for turn in range(1, auxs):
                for c in range(cols):
                    near_copy(g, turn, c).wait_send()

            @pl.when(g < AHEAD)
            def _():
                g_move.z_own(g)

            g_move.r_start(g)

        @when(j >= 3, lax.rem(j, 2) == 1)
        def _():
            p = EARLY + lax.div(j - 3, 2)

            @pl.when(p < PIECES)
            def _():
                d_sends(p, row != me)

        @when(j >= 1, j < 3)
        def _():
            b_move.r_forward(PIECES - 3 + j)

        @when(j >= 3 + passes)
        def _():
            g_move.r_forward(j - 3 - passes)

    g_passed = PIECES - passes
    f_load.wait()
    for q in range(spare, chunks):
        for t in range(tiles):
            upd_fetch(q, t).start()

    @pl.loop(0, PIECES)
    def _(p):
        b_move.r_finish(p)

    def occ_of(block):
        return eps_occ[occ[block * virt]]

    substeps = max(rows - 1, tiles)

    @pl.loop(0, PIECES * substeps)
    def _(n):
        p, t = lax.div(n, substeps), lax.rem(n, substeps)

        @pl.when(t == 0)
        def _():
            g_move.dispatch(row, p, True)

            @pl.when(p + AHEAD < PIECES)
            def _():
                g_move.z_own(p + AHEAD)

        @when(p < LAG, t >= 1)
        def _():
            late = g_passed + p * (substeps - 1) + t - 1

            @pl.when(late < PIECES)
            def _():
                g_move.r_forward(late)

        q = p - LAG

        @when(q == 0, t == 0)
        def _():
            @pl.loop(0, PIECES)
            def _(i):
                g_move.r_finish(i)

            @pl.when(row == me)
            def _():
                d_here.wait()

        @when(q >= 0, t < tiles)
        def _():
            @pl.when(t == 0)
            def _():
                g_move.c_finish(q)
                d_finish(q)

            upd_fetch(q, t).wait()
            rs, cs = tile_rows(t), tile_cols(q)
            held = y.at[q, rs]
            acc = residual(
                held, grow[rs, :], brow[rs, :], frow.at[rs],
                gcol[cs, :], bcol[cs, :], dcol.at[cs], virt,
            )
            delta = pair_sums(
                vsum[...], occ_of,
                row * (height // virt) + t * (FUSED_ROWS // virt), FUSED_ROWS,
                me * (across // virt) + q * (wide // virt), wide,
            )
            y[q, rs, :] = (held[...].astype(f32) - acc / delta).astype(y.dtype)

        @pl.when(t + 1 < rows)
        def _():
            g_move.hop(p, t + 1)

    @pl.loop(PIECES - LAG, PIECES)
    def _(q):
        g_move.c_finish(q)
        d_finish(q)

    @pl.loop(0, PIECES)
    def _(p):
        b_move.sent(p)
        g_move.sent(p)
        for step in range(1, cols):
            far_copy(p, step).wait_send()

        @when(up, row >= me)
        def _():
            d_copy(p, 1, False).wait_send()

        @when(down, row <= me)
        def _():
            d_copy(p, -1, False).wait_send()


def fused(amps, b_loc, fock, occ, virt_at, eps_occ, eps_virt, sizes):
    rows, cols, auxs = sizes
    count = cols * auxs
    height, across = amps.shape
    width, virt = b_loc.shape[1], fock.shape[1]
    full = count * width
    size, wide = height // PIECES, across // PIECES
    tiles = height // FUSED_ROWS
    chunks = PIECES - LAG
    kind = amps.dtype
    any_space = pl.BlockSpec(memory_space=pl.ANY)
    in_smem = pl.BlockSpec(memory_space=pltpu.SMEM)
    in_vmem = pl.BlockSpec(memory_space=pltpu.VMEM)
    hops = (cols - 1) + (auxs - 1) + (cols - 1) * (auxs - 1)
    dma = pltpu.SemaphoreType.DMA
    exchange_sems = [
        dma((2, rows, PIECES)), dma((rows, PIECES)), dma((rows, PIECES)),
        dma((count, PIECES)), dma((hops, PIECES)), dma((count, PIECES)), dma((2, PIECES)),
    ]
    near = max(auxs - 1, 1)
    far = max(cols - 1, 1)

    def shaped(*shape, dtype=kind):
        return jax.ShapeDtypeStruct(shape, dtype)

    return pl.pallas_call(
        functools.partial(fused_kernel, rows, cols, auxs),
        out_shape=(
            pltpu.VMEM((chunks, height, wide), kind),
            pltpu.VMEM((height, full), kind), pltpu.VMEM((height, full), kind),
            pltpu.VMEM((across, full), kind), pltpu.VMEM((across, full), kind),
            pltpu.VMEM((height, virt), kind), pltpu.VMEM((across, virt), kind),
            pltpu.VMEM((virt, virt), jnp.float32),
            shaped(rows, height, width), shaped(rows, height, width),
        ),
        in_specs=[any_space] * 3 + [in_smem] * 4,
        out_specs=(in_vmem,) * 8 + (any_space,) * 2,
        scratch_shapes=[
            pltpu.VMEM((height, width), kind),
            pltpu.VMEM((4, near, cols, size, width), kind),
            pltpu.VMEM((near, cols, height, width), kind),
            pltpu.VMEM((4, cols, size, width), jnp.float32),
            pltpu.VMEM((far, height, width), kind),
            pltpu.VMEM((far, height, width), kind),
            *exchange_sems, *exchange_sems,
            dma((2, PIECES)), dma((PIECES,)),
            dma((near, cols, PIECES)), dma((near, cols, PIECES)),
            dma((far, PIECES)), dma((far, PIECES)),
            dma((2, PIECES)), dma((chunks, tiles)), dma((2,)),
        ],
        compiler_params=pltpu.CompilerParams(
            collective_id=3, has_side_effects=True, vmem_limit_bytes=SCRATCH_BYTES
        ),
        name="fused",
    )(amps, b_loc, fock, occ, virt_at, eps_occ, eps_virt)


def finish_kernel(
    sizes, y, grow, brow, gcol, bcol, frow, dcol, vsum, amps, occ, eps_occ,
    out, held, in_sem, out_sem, move_sem,
):
    cols, auxs = sizes
    row = lax.axis_index("row")
    me = lax.axis_index("col") * auxs + lax.axis_index("aux")
    chunks, height, wide = y.shape
    across = amps.shape[1]
    virt = frow.shape[1]
    tiles = height // FUSED_ROWS
    steps = (across // wide - chunks) * tiles

    def place(n):
        q, t = chunks + lax.div(n, tiles), lax.rem(n, tiles)
        return (
            pl.ds(pl.multiple_of(t * FUSED_ROWS, FUSED_ROWS), FUSED_ROWS),
            pl.ds(pl.multiple_of(q * wide, wide), wide),
        )

    def load(n):
        return pltpu.make_async_copy(amps.at[place(n)], held.at[n], in_sem.at[n])

    def store(n):
        return pltpu.make_async_copy(held.at[n], out.at[place(n)], out_sem.at[n])

    def move(q):
        return pltpu.make_async_copy(
            y.at[q], out.at[:, pl.ds(q * wide, wide)], move_sem.at[q]
        )

    for n in range(steps):
        load(n).start()
    for q in range(chunks):
        move(q).start()

    def occ_of(block):
        return eps_occ[occ[block * virt]]

    @pl.loop(0, steps)
    def _(n):
        q, t = chunks + lax.div(n, tiles), lax.rem(n, tiles)
        rs, cs = place(n)
        load(n).wait()
        tile = held.at[n]
        acc = residual(
            tile, grow[rs, :], brow[rs, :], frow.at[rs],
            gcol[cs, :], bcol[cs, :], dcol.at[cs], virt,
        )
        delta = pair_sums(
            vsum[...], occ_of,
            row * (height // virt) + t * (FUSED_ROWS // virt), FUSED_ROWS,
            me * (across // virt) + q * (wide // virt), wide,
        )
        held[n] = (tile[...].astype(jnp.float32) - acc / delta).astype(held.dtype)
        store(n).start()

    for n in range(steps):
        store(n).wait()
    for q in range(chunks):
        move(q).wait()


def finish(y, kept, amps, occ, eps_occ, sizes):
    chunks, height, wide = y.shape
    steps = (amps.shape[1] // wide - chunks) * (height // FUSED_ROWS)
    here = [pltpu.with_memory_space_constraint(x, pltpu.VMEM) for x in (y, *kept)]
    any_space = pl.BlockSpec(memory_space=pl.ANY)
    in_smem = pl.BlockSpec(memory_space=pltpu.SMEM)
    in_vmem = pl.BlockSpec(memory_space=pltpu.VMEM)
    return pl.pallas_call(
        functools.partial(finish_kernel, sizes[1:]),
        out_shape=jax.ShapeDtypeStruct(amps.shape, amps.dtype),
        in_specs=[in_vmem] * len(here) + [any_space, in_smem, in_smem],
        out_specs=any_space,
        scratch_shapes=[
            pltpu.VMEM((steps, FUSED_ROWS, wide), amps.dtype),
            pltpu.SemaphoreType.DMA((steps,)),
            pltpu.SemaphoreType.DMA((steps,)),
            pltpu.SemaphoreType.DMA((chunks,)),
        ],
        compiler_params=pltpu.CompilerParams(vmem_limit_bytes=SCRATCH_BYTES),
        name="finish",
    )(*here, amps, occ, eps_occ)


def fits(sizes, height, across, width, virt):
    rows, cols, auxs = sizes
    return (
        rows == cols * auxs
        and width % LANES == 0
        and height % (4 * FUSED_ROWS) == 0
        and across % (PIECES * virt) == 0
        and rows > 1 and cols > 1 and auxs > 1
    )


def body(sizes, amplitudes, b_factors, fock_blocks, occ_index, virt_index, eps_occ, eps_virt):
    height, across = amplitudes.shape
    if not fits(sizes, height, across, b_factors.shape[1], fock_blocks.shape[1]):
        return staged_body(
            sizes, amplitudes, b_factors, fock_blocks, occ_index, virt_index, eps_occ, eps_virt
        )
    y, *kept, _, _ = fused(
        amplitudes, b_factors, fock_blocks, occ_index, virt_index, eps_occ, eps_virt, sizes
    )
    return finish(y, kept, amplitudes, occ_index, eps_occ, sizes)


def solution(mesh):
    in_specs = (
        P(("groups", "row"), ("col", "aux")),
        P(("groups", "row"), ("col", "aux")),
        P(("groups", "row"), None),
        P("groups"),
        P("groups"),
        P("groups"),
        P("groups"),
    )
    out_specs = P(("groups", "row"), ("col", "aux"))
    sizes = (mesh.shape["row"], mesh.shape["col"], mesh.shape["aux"])
    return jax.shard_map(
        functools.partial(body, sizes),
        mesh=mesh, in_specs=in_specs, out_specs=out_specs, check_vma=False,
    )
```
